32 devices in a mesh: groups: 2 (over y), row: 8 (over z, x), col: 2 (over core).
Axes of the slice: x: 2, y: 2, z: 4, core: 2. Of those that a mesh axis runs over, the one named last changes fastest.
Arguments:
- queries: float32 [128, 4096], P(('groups', 'row'), 'col'), parts along dimension 0, may hold values from -3 to 3
- documents: float32 [128, 4096], P(('groups', 'row'), 'col'), parts along dimension 0, may hold values from -3 to 3
- positive: int32 [128], P(('groups', 'row')), parts along dimension 0, may hold values from 0 to 63, as said below
- hard_ids: int32 [128, 7], P(('groups', 'row')), parts along dimension 0, may hold values from 0 to 63
Outputs:
- request_derivative: float32 [128, 4096], P(('groups', 'row'), 'col'), parts along dimension 0
- passage_derivative: float32 [128, 4096], P(('groups', 'row'), 'col'), parts along dimension 0
- loss_rows: float32 [128], P(('groups', 'row')), parts along dimension 0
The draws below stay inside these ranges and needn't reach their ends.
There are 2 independent parts, one for each index of `groups`. The reference program is written for one: setup_inputs(seed, part) draws one part's arguments, and reference() takes and returns one part's arrays. A program takes and returns all parts, laid end to end along the dimension named above; each array names one. Nothing has to cross between parts.
Inputs may be any that keep to these rules, and one draw needn't show every extreme that they name: positive[i] is a document of query i's own aligned block of 8, from i - i % 8 to i - i % 8 + 7; within each block every document is the positive of exactly one query.
All inputs are finite; a program needn't handle non-finite values.
Results may differ from the reference program's by a relative error of at most 0.006.
Values may be sent and summed in bfloat16 or wider, within the bound.
No kernel may reach another device: no remote copies, remote signals or barrier semaphores. Data moves between devices by JAX's collectives and lax.ppermute only.
A program may use at most 64 MiB of HBM per device.

```python
import jax
import jax.numpy as jnp

LATENT_DIMENSION = 4096
ROWS = 8
HARD = 7
BATCH = 64


doc_level = 0.24


peak_level = 0.53


shared_level = 0.24


flat_noise = 0.08


def positive_table(key):
    blocks = BATCH // ROWS
    keys = jax.random.split(jax.random.fold_in(key, 11), blocks)
    orders = jax.vmap(lambda single: jax.random.permutation(single, ROWS))(keys)
    starts = jnp.arange(blocks, dtype=jnp.int32)[:, None] * ROWS
    return (orders.astype(jnp.int32) + starts).reshape(BATCH)


def doc_table(key):
    width_scale = LATENT_DIMENSION ** (-0.25)
    doc_sigma = doc_level * width_scale
    base = jnp.clip(jax.random.normal(jax.random.fold_in(key, 21), (BATCH, LATENT_DIMENSION), jnp.float32), -5.0, 5.0) * doc_sigma
    return base


def draw_documents(key, part):
    return doc_table(key)


def draw_positive(key, part):
    return positive_table(key)


def draw_queries(key, part):
    width_scale = LATENT_DIMENSION ** (-0.25)
    peaked = jnp.clip(jax.random.normal(jax.random.fold_in(key, 31), (BATCH, LATENT_DIMENSION), jnp.float32), -4.0, 4.0) * (peak_level * width_scale)
    shared = jnp.clip(jax.random.normal(jax.random.fold_in(key, 34), (1, LATENT_DIMENSION), jnp.float32), -4.0, 4.0) * (shared_level * width_scale)
    jitter = jnp.clip(jax.random.normal(jax.random.fold_in(key, 35), (BATCH, LATENT_DIMENSION), jnp.float32), -4.0, 4.0) * (flat_noise * width_scale)
    flat = shared + jitter
    flat_rows = jax.random.bernoulli(jax.random.fold_in(key, 36), 0.5, (BATCH, 1))
    return jnp.where(flat_rows, flat, peaked)


def with_ends(values, rng, least, top_value):
    extent = values.shape
    index_at = [jax.random.randint(jax.random.fold_in(rng, axis), (), 0, extent[axis]) for axis in range(len(extent))]
    values = values.at[tuple(index_at)].set(least)
    longest = extent.index(max(extent))
    index_at[longest] = (index_at[longest] + 1) % extent[longest]
    return values.at[tuple(index_at)].set(top_value)


def setup_inputs(seed: int = 0, part: int = 0) -> dict:
    splits = jax.random.split(jax.random.key(seed), 5)
    part_keys = jax.random.split(jax.random.fold_in(splits[4], part), 5)
    queries = draw_queries(jax.random.fold_in(jax.random.fold_in(splits[4], part), 71), part)
    documents = draw_documents(jax.random.fold_in(jax.random.fold_in(splits[4], part), 71), part)
    positive = draw_positive(jax.random.fold_in(jax.random.fold_in(splits[4], part), 71), part)
    hard_ids = with_ends(jax.random.randint(part_keys[3], (BATCH, HARD), 0, BATCH), jax.random.fold_in(part_keys[3], 1), 0, BATCH - 1).astype(jnp.int32)
    return dict(queries=queries, documents=documents, positive=positive, hard_ids=hard_ids)


sharpness_divisor = 0.05
hardness_multiplier = 3.0


def weigh(request_similarity, passage_similarity, positive, hard_ids, batch_size):
    columns = jnp.arange(batch_size, dtype=jnp.int32)
    hardness_tally = jnp.zeros(request_similarity.shape, jnp.float32)
    for column in range(hard_ids.shape[1]):
        hardness_tally = hardness_tally + (hard_ids[:, column][:, None] == columns[None, :]).astype(jnp.float32)
    request_raw_similarity = request_similarity / sharpness_divisor + jnp.log1p(hardness_multiplier * hardness_tally)
    matching_indicator = positive[:, None] == columns[None, :]
    passage_raw_similarity = jnp.where(matching_indicator, -jnp.inf, passage_similarity / sharpness_divisor)
    row_peak = jnp.maximum(jnp.max(request_raw_similarity, axis=1), jnp.max(passage_raw_similarity, axis=1))
    row_mass = jnp.sum(jnp.exp(request_raw_similarity - row_peak[:, None]), axis=1) + jnp.sum(jnp.exp(passage_raw_similarity - row_peak[:, None]), axis=1)
    row_lse = row_peak + jnp.log(row_mass)
    loss_rows = row_lse - jnp.sum(jnp.where(matching_indicator, request_raw_similarity, 0.0), axis=1)
    request_probability = jnp.exp(request_raw_similarity - row_lse[:, None]).astype(jnp.bfloat16)
    passage_probability = jnp.exp(passage_raw_similarity - row_lse[:, None]).astype(jnp.bfloat16)
    return request_probability, passage_probability, loss_rows


def reference(queries, documents, positive, hard_ids):
    batch_size = documents.shape[0]
    request_matrix = queries.astype(jnp.bfloat16)
    passage_matrix = documents.astype(jnp.bfloat16)
    reference_side_entries = jnp.take(passage_matrix, positive, axis=0)
    request_similarity = jnp.dot(request_matrix, passage_matrix.T, preferred_element_type=jnp.float32)
    passage_similarity = jnp.dot(reference_side_entries, passage_matrix.T, preferred_element_type=jnp.float32)
    request_probability, passage_probability, loss_rows = weigh(request_similarity, passage_similarity, positive, hard_ids, batch_size)
    request_derivative = (jnp.dot(request_probability, passage_matrix, preferred_element_type=jnp.float32) - reference_side_entries.astype(jnp.float32)) / sharpness_divisor
    reference_side_derivative = jnp.dot(passage_probability, passage_matrix, preferred_element_type=jnp.float32) / sharpness_divisor
    forwarded_entries = reference_side_derivative - request_matrix.astype(jnp.float32) / sharpness_divisor
    dispersion_level = jnp.zeros(documents.shape, jnp.float32).at[positive].add(forwarded_entries)
    aggregate_loss = jnp.dot(request_probability.T, request_matrix, preferred_element_type=jnp.float32) + jnp.dot(passage_probability.T, reference_side_entries, preferred_element_type=jnp.float32)
    passage_derivative = aggregate_loss / sharpness_divisor + dispersion_level
    return request_derivative, passage_derivative, loss_rows
```

```python
import functools

import jax
import jax.numpy as jnp
from jax import lax
from jax.experimental import pallas as pl
from jax.experimental.pallas import tpu as pltpu
from jax.sharding import PartitionSpec as P

sharpness_divisor = 0.05
hardness_multiplier = 3.0
LANES = 128
VMEM = pl.BlockSpec(memory_space=pltpu.VMEM)
SMEM = pl.BlockSpec(memory_space=pltpu.SMEM)
HBM = pl.BlockSpec(memory_space=pltpu.HBM)
PARAMS = pltpu.CompilerParams(vmem_limit_bytes=8 << 20)


def slot_matrix(positive_ref, rows):
    slots = lax.broadcasted_iota(jnp.int32, (rows, rows), 0)
    places = lax.broadcasted_iota(jnp.int32, (rows, rows), 1)
    hit = jnp.zeros((rows, rows), jnp.float32)
    for i in range(rows):
        local = lax.rem(positive_ref[i], rows)
        hit = jnp.where((places == i) & (slots == local), 1.0, hit)
    return hit


def pack_kernel(
    positive_hbm, query_hbm, doc_hbm, hard_hbm, out_ref, positive_ref, query_ref, doc_ref, hard_ref, sems
):
    copies = [
        pltpu.make_async_copy(source, target, sems.at[n])
        for n, (source, target) in enumerate(
            (
                (positive_hbm, positive_ref),
                (query_hbm, query_ref),
                (doc_hbm, doc_ref),
                (hard_hbm, hard_ref),
            )
        )
    ]
    for copy in copies:
        copy.start()
    for copy in copies:
        copy.wait()
    rows, width = query_ref.shape
    tail = out_ref.shape[1] - width
    hit = slot_matrix(positive_ref, rows)
    queries = jnp.dot(
        hit.astype(jnp.bfloat16),
        query_ref[...].astype(jnp.bfloat16),
        preferred_element_type=jnp.float32,
    )
    lane = lax.broadcasted_iota(jnp.int32, (rows, tail), 1)
    block, place = lane // (2 * rows), lax.rem(lane, 2 * rows)
    column = jnp.where(place >= rows, block * rows + place - rows, -1)
    hard = hard_ref[...]
    counts = jnp.zeros((rows, tail), jnp.float32)
    for k in range(hard.shape[1]):
        counts = counts + jnp.where(hard[:, k][:, None] == column, 1.0, 0.0)
    counts = jnp.dot(
        hit.astype(jnp.bfloat16), counts.astype(jnp.bfloat16), preferred_element_type=jnp.float32
    )
    upper = jnp.concatenate([queries, counts], axis=1)
    lower = jnp.concatenate([doc_ref[...], jnp.zeros((rows, tail), jnp.float32)], axis=1)
    out_ref[...] = jnp.concatenate([upper, lower], axis=0).astype(jnp.bfloat16)


def score_kernel(masks, width, *refs):
    *block_refs, all_ref, score_ref = refs
    me = lax.axis_index("row")
    side = lax.axis_index("col")
    for ref, (first, second) in zip(block_refs, masks):
        for n, (a, b) in enumerate(zip(first, second)):
            mask = a if a == b else jnp.where(side == 0, a, b)
            value = ref[...] if len(ref.shape) == 2 else ref[n]
            all_ref[lax.bitwise_xor(me, mask)] = value
    blocks, height, depth = all_ref.shape
    rows = all_ref[...].reshape(blocks * height, depth)[:, :width]
    score_ref[...] = lax.dot_general(
        rows, rows, (((1,), (1,)), ((), ())), preferred_element_type=jnp.float32
    )


def finish_kernel(
    width, positive_ref, own_ref, other_ref, all_ref, request_ref, passage_ref, loss_ref, hold
):
    me = lax.axis_index("row")
    blocks, height, depth = all_ref.shape
    rows, total = height // 2, blocks * height
    scores = (own_ref[...] + other_ref[...]) / sharpness_divisor
    counts = all_ref[...].reshape(total, depth)[:, width:].astype(jnp.float32)
    row = lax.broadcasted_iota(jnp.int32, (total, total), 0)
    lane = lax.broadcasted_iota(jnp.int32, (total, total), 1)
    is_document = lax.rem(lane, height) >= rows
    logits = jnp.where(
        is_document & (row != lane), scores + jnp.log1p(hardness_multiplier * counts), -jnp.inf
    ).reshape(blocks, 2, rows, total)
    peak = jnp.max(jnp.max(logits, axis=1), axis=-1, keepdims=True)
    mass = jnp.sum(jnp.sum(jnp.exp(logits - peak[:, None]), axis=1), axis=-1, keepdims=True)
    lse = peak + jnp.log(mass)
    weights = jnp.exp(logits - lse[:, None]).reshape(total, total)
    hold[0] = weights.reshape(blocks, height, total)
    hold[1] = weights.T.reshape(blocks, height, total)
    hold[2] = logits.reshape(blocks, height, total)
    hit = slot_matrix(positive_ref, rows)
    back = hit.T.astype(jnp.bfloat16)
    mine = hold[0, me].astype(jnp.bfloat16)
    onto = hold[1, me].astype(jnp.bfloat16)
    request_weights = jnp.dot(back, mine[:rows], preferred_element_type=jnp.float32).astype(jnp.bfloat16)
    left = jnp.concatenate([request_weights, mine[rows:], onto], axis=0)
    values = all_ref[...].reshape(total, depth)[:, :width]
    product = jnp.dot(left, values, preferred_element_type=jnp.float32)
    block = all_ref[me]
    anchors = jnp.dot(back, block[rows:, :width], preferred_element_type=jnp.float32)
    request_ref[...] = (product[:rows] - anchors) / sharpness_divisor
    passage_ref[...] = (
        product[rows : 2 * rows] + product[3 * rows :] - block[:rows, :width].astype(jnp.float32)
    ) / sharpness_divisor
    own_logits = hold[2, me][:rows]
    slot = lax.broadcasted_iota(jnp.int32, (rows, total), 0) + me * height + rows
    at = lax.broadcasted_iota(jnp.int32, (rows, total), 1)
    picked = jnp.sum(jnp.where(slot == at, own_logits, 0.0), axis=1, keepdims=True)
    again = jnp.max(hold[2, me].reshape(2, rows, total), axis=0)
    top = jnp.max(again, axis=1, keepdims=True)
    spread = jnp.exp(hold[2, me].reshape(2, rows, total) - top[None])
    own_lse = top + jnp.log(jnp.sum(jnp.sum(spread, axis=0), axis=1, keepdims=True))
    loss_ref[...] = jnp.sum(hit * (own_lse - picked), axis=0)


def exchange(value, masks):
    count = lax.axis_size("row")
    sides = lax.axis_size("col")
    pairs = [
        (sides * i + c, sides * (i ^ masks[c]) + c) for i in range(count) for c in range(sides)
    ]
    return lax.ppermute(value, ("row", "col"), pairs)


PLAN = (((0,), (1, 4)), ((0, 1), (4, 2)), ((0, 1, 2), (2, 1)))


def on_device_fast(queries, documents, positive, hard_ids):
    rows, width = queries.shape
    count = lax.axis_size("row")
    height, total = 2 * rows, 2 * rows * count
    tail = -(-total // LANES) * LANES
    block = pl.pallas_call(
        pack_kernel,
        out_shape=jax.ShapeDtypeStruct((height, width + tail), jnp.bfloat16),
        in_specs=[HBM, HBM, HBM, HBM],
        out_specs=VMEM,
        scratch_shapes=[
            pltpu.SMEM(positive.shape, positive.dtype),
            pltpu.VMEM(queries.shape, queries.dtype),
            pltpu.VMEM(documents.shape, documents.dtype),
            pltpu.VMEM(hard_ids.shape, hard_ids.dtype),
            pltpu.SemaphoreType.DMA((4,)),
        ],
        compiler_params=PARAMS,
        name="pack",
    )(positive, queries, documents, hard_ids)
    pieces, masks = [block[None]], [([0], [0])]
    for step, (sources, hops) in enumerate(PLAN):
        with jax.named_scope(f"hop{step}"):
            held = [pieces[n] for n in sources]
            held = held[0] if len(held) == 1 else jnp.concatenate(held, axis=0)
            pieces.append(exchange(held, hops))
        masks.append(
            tuple([m ^ hops[c] for n in sources for m in masks[n][c]] for c in range(len(hops)))
        )
    everything, own = pl.pallas_call(
        functools.partial(score_kernel, masks, width),
        out_shape=(
            jax.ShapeDtypeStruct((count, height, width + tail), jnp.bfloat16),
            jax.ShapeDtypeStruct((total, total), jnp.float32),
        ),
        in_specs=[VMEM] * len(pieces),
        out_specs=(VMEM, VMEM),
        compiler_params=PARAMS,
        name="score",
    )(*pieces)
    other = lax.ppermute(own, "col", [(0, 1), (1, 0)])
    return pl.pallas_call(
        functools.partial(finish_kernel, width),
        out_shape=(
            jax.ShapeDtypeStruct((rows, width), jnp.float32),
            jax.ShapeDtypeStruct((rows, width), jnp.float32),
            jax.ShapeDtypeStruct((rows,), jnp.float32),
        ),
        in_specs=[SMEM, VMEM, VMEM, VMEM],
        out_specs=(VMEM, VMEM, VMEM),
        scratch_shapes=[pltpu.VMEM((3, count, height, total), jnp.float32)],
        compiler_params=PARAMS,
        name="finish",
    )(positive, own, other, everything)


def weigh(request_similarity, passage_similarity, positive, hard_ids, batch_size):
    columns = jnp.arange(batch_size, dtype=jnp.int32)
    hardness_tally = jnp.zeros(request_similarity.shape, jnp.float32)
    for column in range(hard_ids.shape[1]):
        hardness_tally = hardness_tally + (hard_ids[:, column][:, None] == columns[None, :]).astype(
            jnp.float32
        )
    request_raw_similarity = request_similarity / sharpness_divisor + jnp.log1p(
        hardness_multiplier * hardness_tally
    )
    matching_indicator = positive[:, None] == columns[None, :]
    passage_raw_similarity = jnp.where(
        matching_indicator, -jnp.inf, passage_similarity / sharpness_divisor
    )
    row_peak = jnp.maximum(
        jnp.max(request_raw_similarity, axis=1), jnp.max(passage_raw_similarity, axis=1)
    )
    row_mass = jnp.sum(jnp.exp(request_raw_similarity - row_peak[:, None]), axis=1) + jnp.sum(
        jnp.exp(passage_raw_similarity - row_peak[:, None]), axis=1
    )
    row_lse = row_peak + jnp.log(row_mass)
    loss_rows = row_lse - jnp.sum(
        jnp.where(matching_indicator, request_raw_similarity, 0.0), axis=1
    )
    request_probability = jnp.exp(request_raw_similarity - row_lse[:, None]).astype(jnp.bfloat16)
    passage_probability = jnp.exp(passage_raw_similarity - row_lse[:, None]).astype(jnp.bfloat16)
    return (request_probability, passage_probability, loss_rows)


def contract_first(left, right):
    return lax.dot_general(
        left, right, (((0,), (0,)), ((), ())), preferred_element_type=jnp.float32
    )


def on_device_wide(queries, documents, positive, hard_ids):
    row_count = queries.shape[0]
    batch_size = row_count * lax.axis_size("row")
    offset = lax.axis_index("row") * row_count
    request_matrix = queries.astype(jnp.bfloat16)
    passage_matrix = documents.astype(jnp.bfloat16)
    local_pos = positive - offset
    picker = local_pos[:, None] == jnp.arange(row_count, dtype=jnp.int32)[None, :]
    reference_side_entries = jnp.take(passage_matrix, local_pos, axis=0)
    document_gathered, query_all = (
        lax.all_gather(passage_matrix, "row", axis=0, tiled=True),
        lax.all_gather(request_matrix, "row", axis=0, tiled=True),
    )
    stacked = jnp.concatenate([request_matrix, reference_side_entries], axis=0)
    partial_value = lax.dot_general(
        stacked, document_gathered, (((1,), (1,)), ((), ())), preferred_element_type=jnp.float32
    )
    query_part = partial_value[:row_count]
    doc_part = partial_value[row_count:]
    request_similarity, passage_similarity = lax.psum((query_part, doc_part), "col")
    request_probability, passage_probability, loss_rows = weigh(
        request_similarity, passage_similarity, positive, hard_ids, batch_size
    )
    request_derivative = (
        jnp.dot(request_probability, document_gathered, preferred_element_type=jnp.float32)
        - reference_side_entries.astype(jnp.float32)
    ) / sharpness_divisor
    reference_side_derivative = (
        jnp.dot(passage_probability, document_gathered, preferred_element_type=jnp.float32)
        / sharpness_divisor
    )
    forwarded_entries = (
        reference_side_derivative - request_matrix.astype(jnp.float32) / sharpness_divisor
    )
    permuted = contract_first(picker.astype(jnp.bfloat16), passage_probability).astype(jnp.bfloat16)
    query_columns, anchor_columns = (
        lax.all_to_all(request_probability, "row", split_axis=1, concat_axis=0, tiled=True),
        lax.all_to_all(permuted, "row", split_axis=1, concat_axis=0, tiled=True),
    )
    anchor_contribution = contract_first(anchor_columns, document_gathered)
    query_contribution = contract_first(query_columns, query_all)
    dispersion_level = lax.dot_general(
        picker.astype(jnp.float32),
        forwarded_entries,
        (((0,), (0,)), ((), ())),
        precision=lax.Precision.HIGHEST,
        preferred_element_type=jnp.float32,
    )
    passage_derivative = (
        query_contribution + anchor_contribution
    ) / sharpness_divisor + dispersion_level
    return (request_derivative, passage_derivative, loss_rows)


def solution(mesh):
    small = mesh.shape["row"] == 8 and mesh.shape["col"] == 2
    return jax.shard_map(
        on_device_fast if small else on_device_wide,
        mesh=mesh,
        in_specs=(
            P(("groups", "row"), "col"),
            P(("groups", "row"), "col"),
            P(("groups", "row")),
            P(("groups", "row"), None),
        ),
        out_specs=(P(("groups", "row"), "col"), P(("groups", "row"), "col"), P(("groups", "row"))),
        check_vma=False,
    )
```

```python
import functools

import jax
import jax.numpy as jnp
from jax import lax
from jax.experimental import pallas as pl
from jax.experimental.pallas import tpu as pltpu
from jax.sharding import PartitionSpec as P


sharpness_divisor = 0.05
hardness_multiplier = 3.0
LANES = 128
VMEM = pl.BlockSpec(memory_space=pltpu.VMEM)
SMEM = pl.BlockSpec(memory_space=pltpu.SMEM)
HBM = pl.BlockSpec(memory_space=pltpu.HBM)
PARAMS = pltpu.CompilerParams(vmem_limit_bytes=8 << 20)


def slot_matrix(positive_ref, rows):
    slots = lax.broadcasted_iota(jnp.int32, (rows, rows), 0)
    places = lax.broadcasted_iota(jnp.int32, (rows, rows), 1)
    hit = jnp.zeros((rows, rows), jnp.float32)
    for i in range(rows):
        local = lax.rem(positive_ref[i], rows)
        hit = jnp.where((places == i) & (slots == local), 1.0, hit)
    return hit


def pack_kernel(
    positive_hbm, query_hbm, doc_hbm, hard_hbm, out_ref, positive_ref, query_ref, doc_ref, hard_ref, sems
):
    copies = [
        pltpu.make_async_copy(source, target, sems.at[n])
        for n, (source, target) in enumerate(
            (
                (positive_hbm, positive_ref),
                (query_hbm, query_ref),
                (doc_hbm, doc_ref),
                (hard_hbm, hard_ref),
            )
        )
    ]
    for copy in copies:
        copy.start()
    for copy in copies:
        copy.wait()
    rows, width = query_ref.shape
    tail = out_ref.shape[1] - width
    hit = slot_matrix(positive_ref, rows)
    queries = jnp.dot(
        hit.astype(jnp.bfloat16),
        query_ref[...].astype(jnp.bfloat16),
        preferred_element_type=jnp.float32,
    )
    lane = lax.broadcasted_iota(jnp.int32, (rows, tail), 1)
    block, place = lane // (2 * rows), lax.rem(lane, 2 * rows)
    column = jnp.where(place >= rows, block * rows + place - rows, -1)
    hard = hard_ref[...]
    counts = jnp.zeros((rows, tail), jnp.float32)
    for k in range(hard.shape[1]):
        counts = counts + jnp.where(hard[:, k][:, None] == column, 1.0, 0.0)
    counts = jnp.dot(
        hit.astype(jnp.bfloat16), counts.astype(jnp.bfloat16), preferred_element_type=jnp.float32
    )
    upper = jnp.concatenate([queries, counts], axis=1)
    lower = jnp.concatenate([doc_ref[...], jnp.zeros((rows, tail), jnp.float32)], axis=1)
    out_ref[...] = jnp.concatenate([upper, lower], axis=0).astype(jnp.bfloat16)


def score_kernel(masks, width, *refs):
    *block_refs, all_ref, score_ref = refs
    me = lax.axis_index("row")
    side = lax.axis_index("col")
    for ref, (first, second) in zip(block_refs, masks):
        for n, (a, b) in enumerate(zip(first, second)):
            mask = a if a == b else jnp.where(side == 0, a, b)
            value = ref[...] if len(ref.shape) == 2 else ref[n]
            all_ref[lax.bitwise_xor(me, mask)] = value
    blocks, height, depth = all_ref.shape
    rows = all_ref[...].reshape(blocks * height, depth)[:, :width]
    score_ref[...] = lax.dot_general(
        rows, rows, (((1,), (1,)), ((), ())), preferred_element_type=jnp.float32
    )


def finish_kernel(
    width, positive_ref, own_ref, other_ref, all_ref, request_ref, passage_ref, loss_ref, hold
):
    me = lax.axis_index("row")
    blocks, height, depth = all_ref.shape
    rows, total = height // 2, blocks * height
    scores = (own_ref[...] + other_ref[...]) / sharpness_divisor
    counts = all_ref[...].reshape(total, depth)[:, width:].astype(jnp.float32)
    row = lax.broadcasted_iota(jnp.int32, (total, total), 0)
    lane = lax.broadcasted_iota(jnp.int32, (total, total), 1)
    is_document = lax.rem(lane, height) >= rows
    logits = jnp.where(
        is_document & (row != lane), scores + jnp.log1p(hardness_multiplier * counts), -jnp.inf
    ).reshape(blocks, 2, rows, total)
    peak = jnp.max(jnp.max(logits, axis=1), axis=-1, keepdims=True)
    mass = jnp.sum(jnp.sum(jnp.exp(logits - peak[:, None]), axis=1), axis=-1, keepdims=True)
    lse = peak + jnp.log(mass)
    weights = jnp.exp(logits - lse[:, None]).reshape(total, total)
    hold[0] = weights.reshape(blocks, height, total)
    hold[1] = weights.T.reshape(blocks, height, total)
    hold[2] = logits.reshape(blocks, height, total)
    hit = slot_matrix(positive_ref, rows)
    back = hit.T.astype(jnp.bfloat16)
    mine = hold[0, me].astype(jnp.bfloat16)
    onto = hold[1, me].astype(jnp.bfloat16)
    request_weights = jnp.dot(back, mine[:rows], preferred_element_type=jnp.float32).astype(jnp.bfloat16)
    left = jnp.concatenate([request_weights, mine[rows:], onto], axis=0)
    values = all_ref[...].reshape(total, depth)[:, :width]
    product = jnp.dot(left, values, preferred_element_type=jnp.float32)
    block = all_ref[me]
    anchors = jnp.dot(back, block[rows:, :width], preferred_element_type=jnp.float32)
    request_ref[...] = (product[:rows] - anchors) / sharpness_divisor
    passage_ref[...] = (
        product[rows : 2 * rows] + product[3 * rows :] - block[:rows, :width].astype(jnp.float32)
    ) / sharpness_divisor
    own_logits = hold[2, me][:rows]
    slot = lax.broadcasted_iota(jnp.int32, (rows, total), 0) + me * height + rows
    at = lax.broadcasted_iota(jnp.int32, (rows, total), 1)
    picked = jnp.sum(jnp.where(slot == at, own_logits, 0.0), axis=1, keepdims=True)
    again = jnp.max(hold[2, me].reshape(2, rows, total), axis=0)
    top = jnp.max(again, axis=1, keepdims=True)
    spread = jnp.exp(hold[2, me].reshape(2, rows, total) - top[None])
    own_lse = top + jnp.log(jnp.sum(jnp.sum(spread, axis=0), axis=1, keepdims=True))
    loss_ref[...] = jnp.sum(hit * (own_lse - picked), axis=0)


def exchange(value, masks):
    count = lax.axis_size("row")
    sides = lax.axis_size("col")
    pairs = [
        (sides * i + c, sides * (i ^ masks[c]) + c) for i in range(count) for c in range(sides)
    ]
    return lax.ppermute(value, ("row", "col"), pairs)


PLAN = [((0,), (4, 4)), ((0,), (2, 2)), ((0,), (1, 1)), ((0, 1), (3, 3)), ((1,), (1, 1)), ((1,), (2, 2))]


def on_device_fast(queries, documents, positive, hard_ids):
    rows, width = queries.shape
    count = lax.axis_size("row")
    height, total = 2 * rows, 2 * rows * count
    tail = -(-total // LANES) * LANES
    block = pl.pallas_call(
        pack_kernel,
        out_shape=jax.ShapeDtypeStruct((height, width + tail), jnp.bfloat16),
        in_specs=[HBM, HBM, HBM, HBM],
        out_specs=VMEM,
        scratch_shapes=[
            pltpu.SMEM(positive.shape, positive.dtype),
            pltpu.VMEM(queries.shape, queries.dtype),
            pltpu.VMEM(documents.shape, documents.dtype),
            pltpu.VMEM(hard_ids.shape, hard_ids.dtype),
            pltpu.SemaphoreType.DMA((4,)),
        ],
        compiler_params=PARAMS,
        name="pack",
    )(*(pltpu.with_memory_space_constraint(v, pltpu.HBM) for v in (positive, queries, documents, hard_ids)))
    pieces, masks = [block[None]], [([0], [0])]
    for sources, hops in PLAN:
        held = [pieces[n] for n in sources]
        held = held[0] if len(held) == 1 else jnp.concatenate(held, axis=0)
        pieces.append(exchange(held, hops))
        masks.append(
            tuple([m ^ hops[c] for n in sources for m in masks[n][c]] for c in range(len(hops)))
        )
    everything, own = pl.pallas_call(
        functools.partial(score_kernel, masks, width),
        out_shape=(
            jax.ShapeDtypeStruct((count, height, width + tail), jnp.bfloat16),
            jax.ShapeDtypeStruct((total, total), jnp.float32),
        ),
        in_specs=[VMEM] * len(pieces),
        out_specs=(VMEM, VMEM),
        compiler_params=PARAMS,
        name="score",
    )(*pieces)
    other = lax.ppermute(own, "col", [(0, 1), (1, 0)])
    return pl.pallas_call(
        functools.partial(finish_kernel, width),
        out_shape=(
            jax.ShapeDtypeStruct((rows, width), jnp.float32),
            jax.ShapeDtypeStruct((rows, width), jnp.float32),
            jax.ShapeDtypeStruct((rows,), jnp.float32),
        ),
        in_specs=[SMEM, VMEM, VMEM, VMEM],
        out_specs=(VMEM, VMEM, VMEM),
        scratch_shapes=[pltpu.VMEM((3, count, height, total), jnp.float32)],
        compiler_params=PARAMS,
        name="finish",
    )(positive, own, other, everything)


def weigh(request_similarity, passage_similarity, positive, hard_ids, batch_size):
    columns = jnp.arange(batch_size, dtype=jnp.int32)
    hardness_tally = jnp.zeros(request_similarity.shape, jnp.float32)
    for column in range(hard_ids.shape[1]):
        hardness_tally = hardness_tally + (hard_ids[:, column][:, None] == columns[None, :]).astype(
            jnp.float32
        )
    request_raw_similarity = request_similarity / sharpness_divisor + jnp.log1p(
        hardness_multiplier * hardness_tally
    )
    matching_indicator = positive[:, None] == columns[None, :]
    passage_raw_similarity = jnp.where(
        matching_indicator, -jnp.inf, passage_similarity / sharpness_divisor
    )
    row_peak = jnp.maximum(
        jnp.max(request_raw_similarity, axis=1), jnp.max(passage_raw_similarity, axis=1)
    )
    row_mass = jnp.sum(jnp.exp(request_raw_similarity - row_peak[:, None]), axis=1) + jnp.sum(
        jnp.exp(passage_raw_similarity - row_peak[:, None]), axis=1
    )
    row_lse = row_peak + jnp.log(row_mass)
    loss_rows = row_lse - jnp.sum(
        jnp.where(matching_indicator, request_raw_similarity, 0.0), axis=1
    )
    request_probability = jnp.exp(request_raw_similarity - row_lse[:, None]).astype(jnp.bfloat16)
    passage_probability = jnp.exp(passage_raw_similarity - row_lse[:, None]).astype(jnp.bfloat16)
    return (request_probability, passage_probability, loss_rows)


def contract_first(left, right):
    return lax.dot_general(
        left, right, (((0,), (0,)), ((), ())), preferred_element_type=jnp.float32
    )


def on_device_wide(queries, documents, positive, hard_ids):
    row_count = queries.shape[0]
    batch_size = row_count * lax.axis_size("row")
    offset = lax.axis_index("row") * row_count
    request_matrix = queries.astype(jnp.bfloat16)
    passage_matrix = documents.astype(jnp.bfloat16)
    local_pos = positive - offset
    picker = local_pos[:, None] == jnp.arange(row_count, dtype=jnp.int32)[None, :]
    reference_side_entries = jnp.take(passage_matrix, local_pos, axis=0)
    document_gathered, query_all = (
        lax.all_gather(passage_matrix, "row", axis=0, tiled=True),
        lax.all_gather(request_matrix, "row", axis=0, tiled=True),
    )
    stacked = jnp.concatenate([request_matrix, reference_side_entries], axis=0)
    partial_value = lax.dot_general(
        stacked, document_gathered, (((1,), (1,)), ((), ())), preferred_element_type=jnp.float32
    )
    query_part = partial_value[:row_count]
    doc_part = partial_value[row_count:]
    request_similarity, passage_similarity = lax.psum((query_part, doc_part), "col")
    request_probability, passage_probability, loss_rows = weigh(
        request_similarity, passage_similarity, positive, hard_ids, batch_size
    )
    request_derivative = (
        jnp.dot(request_probability, document_gathered, preferred_element_type=jnp.float32)
        - reference_side_entries.astype(jnp.float32)
    ) / sharpness_divisor
    reference_side_derivative = (
        jnp.dot(passage_probability, document_gathered, preferred_element_type=jnp.float32)
        / sharpness_divisor
    )
    forwarded_entries = (
        reference_side_derivative - request_matrix.astype(jnp.float32) / sharpness_divisor
    )
    permuted = contract_first(picker.astype(jnp.bfloat16), passage_probability).astype(jnp.bfloat16)
    query_columns, anchor_columns = (
        lax.all_to_all(request_probability, "row", split_axis=1, concat_axis=0, tiled=True),
        lax.all_to_all(permuted, "row", split_axis=1, concat_axis=0, tiled=True),
    )
    anchor_contribution = contract_first(anchor_columns, document_gathered)
    query_contribution = contract_first(query_columns, query_all)
    dispersion_level = lax.dot_general(
        picker.astype(jnp.float32),
        forwarded_entries,
        (((0,), (0,)), ((), ())),
        precision=lax.Precision.HIGHEST,
        preferred_element_type=jnp.float32,
    )
    passage_derivative = (
        query_contribution + anchor_contribution
    ) / sharpness_divisor + dispersion_level
    return (request_derivative, passage_derivative, loss_rows)


def solution(mesh):
    small = mesh.shape["row"] == 8 and mesh.shape["col"] == 2
    return jax.shard_map(
        on_device_fast if small else on_device_wide,
        mesh=mesh,
        in_specs=(
            P(("groups", "row"), "col"),
            P(("groups", "row"), "col"),
            P(("groups", "row")),
            P(("groups", "row"), None),
        ),
        out_specs=(P(("groups", "row"), "col"), P(("groups", "row"), "col"), P(("groups", "row"))),
        check_vma=False,
    )
```

```python
import functools

import jax
import jax.numpy as jnp
from jax import lax
from jax.experimental import pallas as pl
from jax.experimental.pallas import tpu as pltpu
from jax.sharding import PartitionSpec as P


sharpness_divisor = 0.05
hardness_multiplier = 3.0
scale = 1.0 / sharpness_divisor
LANES = 128
VMEM = pl.BlockSpec(memory_space=pltpu.VMEM)
SMEM = pl.BlockSpec(memory_space=pltpu.SMEM)
HBM = pl.BlockSpec(memory_space=pltpu.HBM)
PARAMS = pltpu.CompilerParams(vmem_limit_bytes=8 << 20)


def slot_matrix(positive_ref, rows):
    slots = lax.broadcasted_iota(jnp.int32, (rows, rows), 0)
    places = lax.broadcasted_iota(jnp.int32, (rows, rows), 1)
    hit = jnp.zeros((rows, rows), jnp.float32)
    for i in range(rows):
        local = lax.rem(positive_ref[i], rows)
        hit = jnp.where((places == i) & (slots == local), 1.0, hit)
    return hit


def pack_kernel(
    positive_hbm,
    query_hbm,
    doc_hbm,
    hard_hbm,
    out_ref,
    hit_ref,
    positive_ref,
    query_ref,
    doc_ref,
    hard_ref,
    sems,
):
    copies = [
        pltpu.make_async_copy(source, target, sems.at[n])
        for n, (source, target) in enumerate(
            (
                (positive_hbm, positive_ref),
                (query_hbm, query_ref),
                (doc_hbm, doc_ref),
                (hard_hbm, hard_ref),
            )
        )
    ]
    for copy in copies:
        copy.start()
    for copy in copies:
        copy.wait()
    rows, width = query_ref.shape
    tail = out_ref.shape[1] - width
    hit = slot_matrix(positive_ref, rows)
    hit_ref[...] = hit
    queries = jnp.dot(
        hit.astype(jnp.bfloat16),
        query_ref[...].astype(jnp.bfloat16),
        preferred_element_type=jnp.float32,
    )
    lane = lax.broadcasted_iota(jnp.int32, (rows, tail), 1)
    block, place = lane // (2 * rows), lax.rem(lane, 2 * rows)
    column = jnp.where(place >= rows, block * rows + place - rows, -1)
    hard = hard_ref[...]
    counts = jnp.zeros((rows, tail), jnp.float32)
    for k in range(hard.shape[1]):
        counts = counts + jnp.where(hard[:, k][:, None] == column, 1.0, 0.0)
    counts = jnp.dot(
        hit.astype(jnp.bfloat16), counts.astype(jnp.bfloat16), preferred_element_type=jnp.float32
    )
    upper = jnp.concatenate([queries, counts], axis=1)
    lower = jnp.concatenate([doc_ref[...], jnp.zeros((rows, tail), jnp.float32)], axis=1)
    out_ref[...] = jnp.concatenate([upper, lower], axis=0).astype(jnp.bfloat16)


def score_kernel(masks, width, *refs):
    *block_refs, all_ref, score_ref, hold = refs
    me = lax.axis_index("row")
    side = lax.axis_index("col")
    for ref, (first, second) in zip(block_refs, masks):
        for n, (a, b) in enumerate(zip(first, second)):
            mask = a if a == b else jnp.where(side == 0, a, b)
            all_ref[lax.bitwise_xor(me, mask)] = ref[n]
    blocks, height, depth = all_ref.shape
    rows = height // 2
    values = all_ref[...].reshape(blocks * height, depth)[:, :width]
    product = lax.dot_general(
        values, values, (((1,), (1,)), ((), ())), preferred_element_type=jnp.float32
    ).reshape(blocks, height, blocks * height)
    hold[...] = product
    score_ref[: blocks * rows] = product[:, rows:].reshape(blocks * rows, blocks * height)
    score_ref[blocks * rows :] = hold[me, :rows]


def bias_kernel(width, hit_ref, all_ref, turned_ref, mine_ref, request_ref, passage_ref, hold):
    me = lax.axis_index("row")
    blocks, height, depth = all_ref.shape
    rows, total = height // 2, blocks * height
    counts = all_ref[...].reshape(total, depth)[:, width : width + total].astype(jnp.float32)
    row = lax.broadcasted_iota(jnp.int32, (total, total), 0)
    lane = lax.broadcasted_iota(jnp.int32, (total, total), 1)
    bias = jnp.where(
        (lax.rem(lane, height) >= rows) & (row != lane),
        jnp.log1p(hardness_multiplier * counts),
        -jnp.inf,
    )
    hold[...] = bias.reshape(blocks, height, total)
    mine_ref[...] = hold[me]
    turned_ref[...] = bias.T.reshape(blocks, height, total)[:, rows:].reshape(blocks * rows, total)
    block = all_ref[me]
    back = hit_ref[...].T.astype(jnp.bfloat16)
    anchors = jnp.dot(back, block[rows:, :width], preferred_element_type=jnp.float32)
    request_ref[...] = anchors * -scale
    passage_ref[...] = block[:rows, :width].astype(jnp.float32) * -scale


def finish_kernel(
    width,
    pieces,
    hit_ref,
    own_ref,
    other_ref,
    turned_ref,
    mine_ref,
    request_base,
    passage_base,
    all_ref,
    request_hbm,
    passage_hbm,
    loss_hbm,
    request_ref,
    passage_ref,
    loss_ref,
    sems,
):
    me = lax.axis_index("row")
    blocks, height, _ = all_ref.shape
    rows, total = height // 2, blocks * height
    documents = blocks * rows
    turned = (own_ref[:documents] + other_ref[:documents]) * scale + turned_ref[...]
    is_document = lax.rem(lax.broadcasted_iota(jnp.int32, (1, total), 1), height) >= rows

    def partner(value):
        return jnp.where(
            is_document, jnp.roll(value, rows, axis=1), jnp.roll(value, -rows, axis=1)
        )

    top = jnp.max(turned, axis=0, keepdims=True)
    top = jnp.maximum(top, partner(top))
    mass = jnp.sum(jnp.exp(turned - top), axis=0, keepdims=True)
    lse = top + jnp.log(mass + partner(mass))
    at = lax.broadcasted_iota(jnp.int32, (rows, total), 1)
    slot = lax.broadcasted_iota(jnp.int32, (rows, total), 0) + me * height
    own_lse = jnp.sum(jnp.where(at == slot, lse, 0.0), axis=1, keepdims=True)
    ours = pl.ds(pl.multiple_of(me * rows, rows), rows)
    query_logits = (own_ref[documents:] + other_ref[documents:]) * scale + mine_ref[:rows]
    document_scores = (own_ref[ours] + other_ref[ours]) * scale
    query_weights = jnp.exp(query_logits - own_lse)
    document_weights = jnp.exp(document_scores + mine_ref[rows:] - own_lse)
    onto = jnp.exp(document_scores + turned_ref[ours] - lse)
    back = hit_ref[...].T.astype(jnp.bfloat16)
    request_weights = jnp.dot(
        back, query_weights.astype(jnp.bfloat16), preferred_element_type=jnp.float32
    )
    left = jnp.concatenate(
        [request_weights, document_weights, onto, jnp.zeros_like(onto)], axis=0
    ).astype(jnp.bfloat16)
    picked = jnp.sum(jnp.where(at == slot + rows, query_logits, 0.0), axis=1, keepdims=True)
    loss_ref[...] = jnp.sum(hit_ref[...] * (own_lse - picked), axis=0)
    copies = [pltpu.make_async_copy(loss_ref, loss_hbm, sems.at[2 * pieces])]
    copies[0].start()
    step = width // pieces
    for n in range(pieces):
        span = pl.ds(n * step, step)
        values = all_ref[:, :, span].reshape(total, step)
        product = jnp.dot(left, values, preferred_element_type=jnp.float32)
        request_ref[:, span] = product[:rows] * scale + request_base[:, span]
        passage_ref[:, span] = (
            product[rows : 2 * rows] + product[2 * rows : 3 * rows]
        ) * scale + passage_base[:, span]
        for k, (source, target) in enumerate(
            ((request_ref, request_hbm), (passage_ref, passage_hbm))
        ):
            copies.append(
                pltpu.make_async_copy(source.at[:, span], target.at[:, span], sems.at[2 * n + k])
            )
            copies[-1].start()
    for copy in copies:
        copy.wait()


def exchange(value, masks):
    count = lax.axis_size("row")
    sides = lax.axis_size("col")
    pairs = [
        (sides * i + c, sides * (i ^ masks[c]) + c) for i in range(count) for c in range(sides)
    ]
    return lax.ppermute(value, ("row", "col"), pairs)


PIECES = 4
PLAN = [((0,), (4, 4)), ((0,), (2, 2)), ((0,), (1, 1)), ((0, 1), (3, 3)), ((1,), (1, 1)), ((1,), (2, 2))]


def on_device_fast(queries, documents, positive, hard_ids):
    rows, width = queries.shape
    count = lax.axis_size("row")
    height, total = 2 * rows, 2 * rows * count
    tail = -(-total // LANES) * LANES
    block, hit = pl.pallas_call(
        pack_kernel,
        out_shape=(
            jax.ShapeDtypeStruct((height, width + tail), jnp.bfloat16),
            jax.ShapeDtypeStruct((rows, rows), jnp.float32),
        ),
        in_specs=[HBM, HBM, HBM, HBM],
        out_specs=(VMEM, VMEM),
        scratch_shapes=[
            pltpu.SMEM(positive.shape, positive.dtype),
            pltpu.VMEM(queries.shape, queries.dtype),
            pltpu.VMEM(documents.shape, documents.dtype),
            pltpu.VMEM(hard_ids.shape, hard_ids.dtype),
            pltpu.SemaphoreType.DMA((4,)),
        ],
        compiler_params=PARAMS,
        name="pack",
    )(*(pltpu.with_memory_space_constraint(v, pltpu.HBM) for v in (positive, queries, documents, hard_ids)))
    pieces, masks = [block[None]], [([0], [0])]
    for sources, hops in PLAN:
        held = [pieces[n] for n in sources]
        held = held[0] if len(held) == 1 else jnp.concatenate(held, axis=0)
        pieces.append(exchange(held, hops))
        masks.append(
            tuple([m ^ hops[c] for n in sources for m in masks[n][c]] for c in range(len(hops)))
        )
    everything, own = pl.pallas_call(
        functools.partial(score_kernel, masks, width),
        out_shape=(
            jax.ShapeDtypeStruct((count, height, width + tail), jnp.bfloat16),
            jax.ShapeDtypeStruct((total // 2 + rows, total), jnp.float32),
        ),
        in_specs=[VMEM] * len(pieces),
        out_specs=(VMEM, VMEM),
        scratch_shapes=[pltpu.VMEM((count, height, total), jnp.float32)],
        compiler_params=PARAMS,
        name="score",
    )(*pieces)
    other = lax.ppermute(own, "col", [(0, 1), (1, 0)])
    turned, mine, request_base, passage_base = pl.pallas_call(
        functools.partial(bias_kernel, width),
        out_shape=(
            jax.ShapeDtypeStruct((total // 2, total), jnp.float32),
            jax.ShapeDtypeStruct((height, total), jnp.float32),
            jax.ShapeDtypeStruct((rows, width), jnp.float32),
            jax.ShapeDtypeStruct((rows, width), jnp.float32),
        ),
        in_specs=[VMEM, VMEM],
        out_specs=(VMEM, VMEM, VMEM, VMEM),
        scratch_shapes=[pltpu.VMEM((count, height, total), jnp.float32)],
        compiler_params=PARAMS,
        name="bias",
    )(hit, everything)
    return pl.pallas_call(
        functools.partial(finish_kernel, width, PIECES),
        out_shape=(
            jax.ShapeDtypeStruct((rows, width), jnp.float32),
            jax.ShapeDtypeStruct((rows, width), jnp.float32),
            jax.ShapeDtypeStruct((rows,), jnp.float32),
        ),
        in_specs=[VMEM] * 8,
        out_specs=(HBM, HBM, HBM),
        scratch_shapes=[
            pltpu.VMEM((rows, width), jnp.float32),
            pltpu.VMEM((rows, width), jnp.float32),
            pltpu.VMEM((rows,), jnp.float32),
            pltpu.SemaphoreType.DMA((2 * PIECES + 1,)),
        ],
        compiler_params=PARAMS,
        name="finish",
    )(hit, own, other, turned, mine, request_base, passage_base, everything)


def weigh(request_similarity, passage_similarity, positive, hard_ids, batch_size):
    columns = jnp.arange(batch_size, dtype=jnp.int32)
    hardness_tally = jnp.zeros(request_similarity.shape, jnp.float32)
    for column in range(hard_ids.shape[1]):
        hardness_tally = hardness_tally + (hard_ids[:, column][:, None] == columns[None, :]).astype(
            jnp.float32
        )
    request_raw_similarity = request_similarity / sharpness_divisor + jnp.log1p(
        hardness_multiplier * hardness_tally
    )
    matching_indicator = positive[:, None] == columns[None, :]
    passage_raw_similarity = jnp.where(
        matching_indicator, -jnp.inf, passage_similarity / sharpness_divisor
    )
    row_peak = jnp.maximum(
        jnp.max(request_raw_similarity, axis=1), jnp.max(passage_raw_similarity, axis=1)
    )
    row_mass = jnp.sum(jnp.exp(request_raw_similarity - row_peak[:, None]), axis=1) + jnp.sum(
        jnp.exp(passage_raw_similarity - row_peak[:, None]), axis=1
    )
    row_lse = row_peak + jnp.log(row_mass)
    loss_rows = row_lse - jnp.sum(
        jnp.where(matching_indicator, request_raw_similarity, 0.0), axis=1
    )
    request_probability = jnp.exp(request_raw_similarity - row_lse[:, None]).astype(jnp.bfloat16)
    passage_probability = jnp.exp(passage_raw_similarity - row_lse[:, None]).astype(jnp.bfloat16)
    return (request_probability, passage_probability, loss_rows)


def contract_first(left, right):
    return lax.dot_general(
        left, right, (((0,), (0,)), ((), ())), preferred_element_type=jnp.float32
    )


def on_device_wide(queries, documents, positive, hard_ids):
    row_count = queries.shape[0]
    batch_size = row_count * lax.axis_size("row")
    offset = lax.axis_index("row") * row_count
    request_matrix = queries.astype(jnp.bfloat16)
    passage_matrix = documents.astype(jnp.bfloat16)
    local_pos = positive - offset
    picker = local_pos[:, None] == jnp.arange(row_count, dtype=jnp.int32)[None, :]
    reference_side_entries = jnp.take(passage_matrix, local_pos, axis=0)
    document_gathered, query_all = (
        lax.all_gather(passage_matrix, "row", axis=0, tiled=True),
        lax.all_gather(request_matrix, "row", axis=0, tiled=True),
    )
    stacked = jnp.concatenate([request_matrix, reference_side_entries], axis=0)
    partial_value = lax.dot_general(
        stacked, document_gathered, (((1,), (1,)), ((), ())), preferred_element_type=jnp.float32
    )
    query_part = partial_value[:row_count]
    doc_part = partial_value[row_count:]
    request_similarity, passage_similarity = lax.psum((query_part, doc_part), "col")
    request_probability, passage_probability, loss_rows = weigh(
        request_similarity, passage_similarity, positive, hard_ids, batch_size
    )
    request_derivative = (
        jnp.dot(request_probability, document_gathered, preferred_element_type=jnp.float32)
        - reference_side_entries.astype(jnp.float32)
    ) / sharpness_divisor
    reference_side_derivative = (
        jnp.dot(passage_probability, document_gathered, preferred_element_type=jnp.float32)
        / sharpness_divisor
    )
    forwarded_entries = (
        reference_side_derivative - request_matrix.astype(jnp.float32) / sharpness_divisor
    )
    permuted = contract_first(picker.astype(jnp.bfloat16), passage_probability).astype(jnp.bfloat16)
    query_columns, anchor_columns = (
        lax.all_to_all(request_probability, "row", split_axis=1, concat_axis=0, tiled=True),
        lax.all_to_all(permuted, "row", split_axis=1, concat_axis=0, tiled=True),
    )
    anchor_contribution = contract_first(anchor_columns, document_gathered)
    query_contribution = contract_first(query_columns, query_all)
    dispersion_level = lax.dot_general(
        picker.astype(jnp.float32),
        forwarded_entries,
        (((0,), (0,)), ((), ())),
        precision=lax.Precision.HIGHEST,
        preferred_element_type=jnp.float32,
    )
    passage_derivative = (
        query_contribution + anchor_contribution
    ) / sharpness_divisor + dispersion_level
    return (request_derivative, passage_derivative, loss_rows)


def solution(mesh):
    small = mesh.shape["row"] == 8 and mesh.shape["col"] == 2
    return jax.shard_map(
        on_device_fast if small else on_device_wide,
        mesh=mesh,
        in_specs=(
            P(("groups", "row"), "col"),
            P(("groups", "row"), "col"),
            P(("groups", "row")),
            P(("groups", "row"), None),
        ),
        out_specs=(P(("groups", "row"), "col"), P(("groups", "row"), "col"), P(("groups", "row"))),
        check_vma=False,
    )
```

```python
import functools

import jax
import jax.numpy as jnp
from jax import lax
from jax.experimental import pallas as pl
from jax.experimental.pallas import tpu as pltpu
from jax.sharding import PartitionSpec as P


sharpness_divisor = 0.05
hardness_multiplier = 3.0
scale = 1.0 / sharpness_divisor
LANES = 128
VMEM = pl.BlockSpec(memory_space=pltpu.VMEM)
SMEM = pl.BlockSpec(memory_space=pltpu.SMEM)
HBM = pl.BlockSpec(memory_space=pltpu.HBM)
PARAMS = pltpu.CompilerParams(vmem_limit_bytes=8 << 20)


def slot_matrix(positive_ref, rows):
    slots = lax.broadcasted_iota(jnp.int32, (rows, rows), 0)
    places = lax.broadcasted_iota(jnp.int32, (rows, rows), 1)
    hit = jnp.zeros((rows, rows), jnp.float32)
    for i in range(rows):
        local = lax.rem(positive_ref[i], rows)
        hit = jnp.where((places == i) & (slots == local), 1.0, hit)
    return hit


def pack_kernel(
    positive_hbm,
    query_hbm,
    doc_hbm,
    hard_hbm,
    out_ref,
    hit_ref,
    positive_ref,
    query_ref,
    doc_ref,
    hard_ref,
    sems,
):
    copies = [
        pltpu.make_async_copy(source, target, sems.at[n])
        for n, (source, target) in enumerate(
            (
                (positive_hbm, positive_ref),
                (query_hbm, query_ref),
                (doc_hbm, doc_ref),
                (hard_hbm, hard_ref),
            )
        )
    ]
    for copy in copies:
        copy.start()
    for copy in copies:
        copy.wait()
    rows, width = query_ref.shape
    tail = out_ref.shape[1] - width
    hit = slot_matrix(positive_ref, rows)
    hit_ref[...] = hit
    lane = lax.broadcasted_iota(jnp.int32, (rows, tail), 1)
    block, place = lane // (2 * rows), lax.rem(lane, 2 * rows)
    column = jnp.where(place >= rows, block * rows + place - rows, -1)
    hard = hard_ref[...]
    counts = jnp.zeros((rows, tail), jnp.float32)
    for k in range(hard.shape[1]):
        counts = counts + jnp.where(hard[:, k][:, None] == column, 1.0, 0.0)
    raw = jnp.concatenate([query_ref[...], counts], axis=1)
    upper = jnp.zeros_like(raw)
    for i in range(rows):
        upper = jnp.where(hit[:, i][:, None] > 0.0, raw[i][None, :], upper)
    lower = jnp.concatenate([doc_ref[...], jnp.zeros((rows, tail), jnp.float32)], axis=1)
    out_ref[...] = jnp.concatenate([upper, lower], axis=0).astype(jnp.bfloat16)


def stack(refs, places, start, stop):
    return jnp.concatenate([refs[p][n, :, start:stop] for p, n in places], axis=0)


def score_kernel(places, width, *refs):
    *block_refs, score_ref = refs
    values = stack(block_refs, places, 0, width)
    product = lax.dot_general(
        values, values, (((1,), (1,)), ((), ())), preferred_element_type=jnp.float32
    )
    height, blocks = block_refs[0].shape[1], len(places)
    rows = height // 2
    by_block = product.reshape(blocks, height, blocks * height)
    score_ref[: blocks * rows] = by_block[:, rows:].reshape(blocks * rows, blocks * height)
    score_ref[blocks * rows :] = product[:rows]


def bias_kernel(places, width, hit_ref, *refs):
    *block_refs, turned_ref, mine_ref, request_ref, passage_ref = refs
    me = lax.axis_index("row")
    height, blocks = block_refs[0].shape[1], len(places)
    rows, total = height // 2, blocks * height
    counts = stack(block_refs, places, width, width + total).astype(jnp.float32)
    row = lax.broadcasted_iota(jnp.int32, (total, total), 0)
    lane = lax.broadcasted_iota(jnp.int32, (total, total), 1)
    bit = 1
    while bit < blocks:
        shift = bit * height
        other = jnp.where(
            (lane // shift) % 2 == 0,
            jnp.roll(counts, -shift, axis=1),
            jnp.roll(counts, shift, axis=1),
        )
        counts = jnp.where((me // bit) % 2 == 1, other, counts)
        bit *= 2
    bias = jnp.where(
        (lax.rem(lane, height) >= rows) & (row != lane),
        jnp.log1p(hardness_multiplier * counts),
        -jnp.inf,
    )
    mine_ref[...] = bias[:height]
    turned_ref[...] = bias.T.reshape(blocks, height, total)[:, rows:].reshape(blocks * rows, total)
    block = block_refs[0]
    back = hit_ref[...].T.astype(jnp.bfloat16)
    anchors = jnp.dot(back, block[0, rows:, :width], preferred_element_type=jnp.float32)
    request_ref[...] = anchors * -scale
    passage_ref[...] = block[0, :rows, :width].astype(jnp.float32) * -scale


def finish_kernel(places, width, pieces, *refs):
    hit_ref, own_ref, other_ref, turned_ref, mine_ref, request_base, passage_base = refs[:7]
    block_refs = refs[7:-7]
    request_hbm, passage_hbm, loss_hbm, request_ref, passage_ref, loss_ref, sems = refs[-7:]
    height, blocks = block_refs[0].shape[1], len(places)
    rows, total = height // 2, blocks * height
    documents = blocks * rows
    scores = (own_ref[...] + other_ref[...]) * scale
    turned = scores[:documents] + turned_ref[...]
    is_document = lax.rem(lax.broadcasted_iota(jnp.int32, (1, total), 1), height) >= rows

    def partner(value):
        return jnp.where(
            is_document, jnp.roll(value, rows, axis=1), jnp.roll(value, -rows, axis=1)
        )

    top = jnp.max(turned, axis=0, keepdims=True)
    top = jnp.maximum(top, partner(top))
    mass = jnp.sum(jnp.exp(turned - top), axis=0, keepdims=True)
    lse = top + jnp.log(mass + partner(mass))
    at = lax.broadcasted_iota(jnp.int32, (rows, total), 1)
    slot = lax.broadcasted_iota(jnp.int32, (rows, total), 0)
    own_lse = jnp.sum(jnp.where(at == slot, lse, 0.0), axis=1, keepdims=True)
    query_logits = scores[documents:] + mine_ref[:rows]
    query_weights = jnp.exp(query_logits - own_lse)
    document_weights = jnp.exp(scores[:rows] + mine_ref[rows:] - own_lse)
    onto = jnp.exp(turned[:rows] - lse)
    back = hit_ref[...].T.astype(jnp.bfloat16)
    request_weights = jnp.dot(
        back, query_weights.astype(jnp.bfloat16), preferred_element_type=jnp.float32
    )
    left = jnp.concatenate(
        [request_weights, document_weights, onto, jnp.zeros_like(onto)], axis=0
    ).astype(jnp.bfloat16)
    copies = []
    step = width // pieces
    for n in range(pieces):
        span = pl.ds(n * step, step)
        values = stack(block_refs, places, n * step, (n + 1) * step)
        product = jnp.dot(left, values, preferred_element_type=jnp.float32)
        request_ref[:, span] = product[:rows] * scale + request_base[:, span]
        passage_ref[:, span] = (
            product[rows : 2 * rows] + product[2 * rows : 3 * rows]
        ) * scale + passage_base[:, span]
        for k, (source, target) in enumerate(
            ((request_ref, request_hbm), (passage_ref, passage_hbm))
        ):
            copies.append(
                pltpu.make_async_copy(source.at[:, span], target.at[:, span], sems.at[2 * n + k])
            )
            copies[-1].start()
    picked = jnp.sum(jnp.where(at == slot + rows, query_logits, 0.0), axis=1, keepdims=True)
    loss_ref[...] = jnp.sum(hit_ref[...] * (own_lse - picked), axis=0)
    copies.append(pltpu.make_async_copy(loss_ref, loss_hbm, sems.at[2 * pieces]))
    copies[-1].start()
    for copy in copies:
        copy.wait()


def exchange(value, mask):
    return lax.ppermute(value, "row", [(i, i ^ mask) for i in range(lax.axis_size("row"))])


PIECES = 4
PLAN = (((0,), 4), ((0,), 2), ((0,), 1), ((0, 1), 3), ((1,), 1), ((1,), 2))


def on_device_fast(queries, documents, positive, hard_ids):
    rows, width = queries.shape
    count = lax.axis_size("row")
    height, total = 2 * rows, 2 * rows * count
    tail = -(-total // LANES) * LANES
    block, hit = pl.pallas_call(
        pack_kernel,
        out_shape=(
            jax.ShapeDtypeStruct((height, width + tail), jnp.bfloat16),
            jax.ShapeDtypeStruct((rows, rows), jnp.float32),
        ),
        in_specs=[HBM, HBM, HBM, HBM],
        out_specs=(VMEM, VMEM),
        scratch_shapes=[
            pltpu.SMEM(positive.shape, positive.dtype),
            pltpu.VMEM(queries.shape, queries.dtype),
            pltpu.VMEM(documents.shape, documents.dtype),
            pltpu.VMEM(hard_ids.shape, hard_ids.dtype),
            pltpu.SemaphoreType.DMA((4,)),
        ],
        compiler_params=PARAMS,
        name="pack",
    )(*(pltpu.with_memory_space_constraint(v, pltpu.HBM) for v in (positive, queries, documents, hard_ids)))
    pieces, distances = [block[None]], [[0]]
    for sources, mask in PLAN:
        held = [pieces[n] for n in sources]
        held = held[0] if len(held) == 1 else jnp.concatenate(held, axis=0)
        pieces.append(exchange(held, mask))
        distances.append([m ^ mask for n in sources for m in distances[n]])
    where = {m: (p, n) for p, found in enumerate(distances) for n, m in enumerate(found)}
    places = [where[m] for m in range(count)]
    own = pl.pallas_call(
        functools.partial(score_kernel, places, width),
        out_shape=jax.ShapeDtypeStruct((total // 2 + rows, total), jnp.float32),
        in_specs=[VMEM] * len(pieces),
        out_specs=VMEM,
        compiler_params=PARAMS,
        name="score",
    )(*pieces)
    other = lax.ppermute(own, "col", [(0, 1), (1, 0)])
    prepared = pl.pallas_call(
        functools.partial(bias_kernel, places, width),
        out_shape=(
            jax.ShapeDtypeStruct((total // 2, total), jnp.float32),
            jax.ShapeDtypeStruct((height, total), jnp.float32),
            jax.ShapeDtypeStruct((rows, width), jnp.float32),
            jax.ShapeDtypeStruct((rows, width), jnp.float32),
        ),
        in_specs=[VMEM] * (1 + len(pieces)),
        out_specs=(VMEM, VMEM, VMEM, VMEM),
        compiler_params=PARAMS,
        name="bias",
    )(hit, *pieces)
    return pl.pallas_call(
        functools.partial(finish_kernel, places, width, PIECES),
        out_shape=(
            jax.ShapeDtypeStruct((rows, width), jnp.float32),
            jax.ShapeDtypeStruct((rows, width), jnp.float32),
            jax.ShapeDtypeStruct((rows,), jnp.float32),
        ),
        in_specs=[VMEM] * (7 + len(pieces)),
        out_specs=(HBM, HBM, HBM),
        scratch_shapes=[
            pltpu.VMEM((rows, width), jnp.float32),
            pltpu.VMEM((rows, width), jnp.float32),
            pltpu.VMEM((rows,), jnp.float32),
            pltpu.SemaphoreType.DMA((2 * PIECES + 1,)),
        ],
        compiler_params=PARAMS,
        name="finish",
    )(hit, own, other, *prepared, *pieces)


def weigh(request_similarity, passage_similarity, positive, hard_ids, batch_size):
    columns = jnp.arange(batch_size, dtype=jnp.int32)
    hardness_tally = jnp.zeros(request_similarity.shape, jnp.float32)
    for column in range(hard_ids.shape[1]):
        hardness_tally = hardness_tally + (hard_ids[:, column][:, None] == columns[None, :]).astype(
            jnp.float32
        )
    request_raw_similarity = request_similarity / sharpness_divisor + jnp.log1p(
        hardness_multiplier * hardness_tally
    )
    matching_indicator = positive[:, None] == columns[None, :]
    passage_raw_similarity = jnp.where(
        matching_indicator, -jnp.inf, passage_similarity / sharpness_divisor
    )
    row_peak = jnp.maximum(
        jnp.max(request_raw_similarity, axis=1), jnp.max(passage_raw_similarity, axis=1)
    )
    row_mass = jnp.sum(jnp.exp(request_raw_similarity - row_peak[:, None]), axis=1) + jnp.sum(
        jnp.exp(passage_raw_similarity - row_peak[:, None]), axis=1
    )
    row_lse = row_peak + jnp.log(row_mass)
    loss_rows = row_lse - jnp.sum(
        jnp.where(matching_indicator, request_raw_similarity, 0.0), axis=1
    )
    request_probability = jnp.exp(request_raw_similarity - row_lse[:, None]).astype(jnp.bfloat16)
    passage_probability = jnp.exp(passage_raw_similarity - row_lse[:, None]).astype(jnp.bfloat16)
    return (request_probability, passage_probability, loss_rows)


def contract_first(left, right):
    return lax.dot_general(
        left, right, (((0,), (0,)), ((), ())), preferred_element_type=jnp.float32
    )


def on_device_wide(queries, documents, positive, hard_ids):
    row_count = queries.shape[0]
    batch_size = row_count * lax.axis_size("row")
    offset = lax.axis_index("row") * row_count
    request_matrix = queries.astype(jnp.bfloat16)
    passage_matrix = documents.astype(jnp.bfloat16)
    local_pos = positive - offset
    picker = local_pos[:, None] == jnp.arange(row_count, dtype=jnp.int32)[None, :]
    reference_side_entries = jnp.take(passage_matrix, local_pos, axis=0)
    document_gathered, query_all = (
        lax.all_gather(passage_matrix, "row", axis=0, tiled=True),
        lax.all_gather(request_matrix, "row", axis=0, tiled=True),
    )
    stacked = jnp.concatenate([request_matrix, reference_side_entries], axis=0)
    partial_value = lax.dot_general(
        stacked, document_gathered, (((1,), (1,)), ((), ())), preferred_element_type=jnp.float32
    )
    query_part = partial_value[:row_count]
    doc_part = partial_value[row_count:]
    request_similarity, passage_similarity = lax.psum((query_part, doc_part), "col")
    request_probability, passage_probability, loss_rows = weigh(
        request_similarity, passage_similarity, positive, hard_ids, batch_size
    )
    request_derivative = (
        jnp.dot(request_probability, document_gathered, preferred_element_type=jnp.float32)
        - reference_side_entries.astype(jnp.float32)
    ) / sharpness_divisor
    reference_side_derivative = (
        jnp.dot(passage_probability, document_gathered, preferred_element_type=jnp.float32)
        / sharpness_divisor
    )
    forwarded_entries = (
        reference_side_derivative - request_matrix.astype(jnp.float32) / sharpness_divisor
    )
    permuted = contract_first(picker.astype(jnp.bfloat16), passage_probability).astype(jnp.bfloat16)
    query_columns, anchor_columns = (
        lax.all_to_all(request_probability, "row", split_axis=1, concat_axis=0, tiled=True),
        lax.all_to_all(permuted, "row", split_axis=1, concat_axis=0, tiled=True),
    )
    anchor_contribution = contract_first(anchor_columns, document_gathered)
    query_contribution = contract_first(query_columns, query_all)
    dispersion_level = lax.dot_general(
        picker.astype(jnp.float32),
        forwarded_entries,
        (((0,), (0,)), ((), ())),
        precision=lax.Precision.HIGHEST,
        preferred_element_type=jnp.float32,
    )
    passage_derivative = (
        query_contribution + anchor_contribution
    ) / sharpness_divisor + dispersion_level
    return (request_derivative, passage_derivative, loss_rows)


def solution(mesh):
    small = mesh.shape["row"] == 8 and mesh.shape["col"] == 2
    return jax.shard_map(
        on_device_fast if small else on_device_wide,
        mesh=mesh,
        in_specs=(
            P(("groups", "row"), "col"),
            P(("groups", "row"), "col"),
            P(("groups", "row")),
            P(("groups", "row"), None),
        ),
        out_specs=(P(("groups", "row"), "col"), P(("groups", "row"), "col"), P(("groups", "row"))),
        check_vma=False,
    )
```

```python
import functools

import jax
import jax.numpy as jnp
from jax import lax
from jax.experimental import pallas as pl
from jax.experimental.pallas import tpu as pltpu
from jax.sharding import PartitionSpec as P


sharpness_divisor = 0.05
hardness_multiplier = 3.0
scale = 1.0 / sharpness_divisor
LANES = 128
VMEM = pl.BlockSpec(memory_space=pltpu.VMEM)
SMEM = pl.BlockSpec(memory_space=pltpu.SMEM)
HBM = pl.BlockSpec(memory_space=pltpu.HBM)
PARAMS = pltpu.CompilerParams(vmem_limit_bytes=8 << 20)


def slot_matrix(positive_ref, rows):
    slots = lax.broadcasted_iota(jnp.int32, (rows, rows), 0)
    places = lax.broadcasted_iota(jnp.int32, (rows, rows), 1)
    hit = jnp.zeros((rows, rows), jnp.float32)
    for i in range(rows):
        local = lax.rem(positive_ref[i], rows)
        hit = jnp.where((places == i) & (slots == local), 1.0, hit)
    return hit


def pack_kernel(
    positive_hbm,
    query_hbm,
    doc_hbm,
    hard_hbm,
    out_ref,
    hit_ref,
    positive_ref,
    query_ref,
    doc_ref,
    hard_ref,
    sems,
):
    rows, width = query_ref.shape
    tail = out_ref.shape[1] - width
    step = width // READS
    spans = [pl.ds(n * step, step) for n in range(READS)]
    pairs = [(positive_hbm, positive_ref), (hard_hbm, hard_ref)]
    for span in spans:
        pairs.append((query_hbm.at[:, span], query_ref.at[:, span]))
        pairs.append((doc_hbm.at[:, span], doc_ref.at[:, span]))
    copies = [
        pltpu.make_async_copy(source, target, sems.at[n]) for n, (source, target) in enumerate(pairs)
    ]
    for copy in copies:
        copy.start()
    copies[0].wait()
    copies[1].wait()
    hit = slot_matrix(positive_ref, rows)
    hit_ref[...] = hit
    chosen = [hit[:, i][:, None] > 0.0 for i in range(rows)]

    def in_slots(value):
        placed = jnp.zeros_like(value)
        for i in range(rows):
            placed = jnp.where(chosen[i], value[i][None, :], placed)
        return placed

    lane = lax.broadcasted_iota(jnp.int32, (rows, tail), 1)
    block, place = lane // (2 * rows), lax.rem(lane, 2 * rows)
    column = jnp.where(place >= rows, block * rows + place - rows, -1)
    hard = hard_ref[...]
    counts = jnp.zeros((rows, tail), jnp.float32)
    for k in range(hard.shape[1]):
        counts = counts + jnp.where(hard[:, k][:, None] == column, 1.0, 0.0)
    out_ref[:, width:] = jnp.concatenate(
        [in_slots(counts), jnp.zeros_like(counts)], axis=0
    ).astype(jnp.bfloat16)
    for n, span in enumerate(spans):
        copies[2 + 2 * n].wait()
        copies[3 + 2 * n].wait()
        out_ref[:, span] = jnp.concatenate(
            [in_slots(query_ref[:, span]), doc_ref[:, span]], axis=0
        ).astype(jnp.bfloat16)


def stack(refs, places, start, stop):
    return jnp.concatenate([refs[p][n, :, start:stop] for p, n in places], axis=0)


def in_order(hit, value):
    back = hit.T
    placed = jnp.zeros_like(value)
    for p in range(value.shape[0]):
        placed = jnp.where(back[:, p][:, None] > 0.0, value[p][None, :], placed)
    return placed


def score_kernel(places, width, hit_ref, *refs):
    *block_refs, score_ref = refs
    values = stack(block_refs, places, 0, width)
    product = lax.dot_general(
        values, values, (((1,), (1,)), ((), ())), preferred_element_type=jnp.float32
    )
    height, blocks = block_refs[0].shape[1], len(places)
    rows = height // 2
    by_block = product.reshape(blocks, height, blocks * height)
    score_ref[: blocks * rows] = by_block[:, rows:].reshape(blocks * rows, blocks * height)
    score_ref[blocks * rows :] = in_order(hit_ref[...], product[:rows])


def bias_kernel(places, width, hit_ref, *refs):
    *block_refs, turned_ref, mine_ref, request_ref, passage_ref = refs
    hit = hit_ref[...]
    me = lax.axis_index("row")
    height, blocks = block_refs[0].shape[1], len(places)
    rows, total = height // 2, blocks * height
    counts = stack(block_refs, places, width, width + total).astype(jnp.float32)
    row = lax.broadcasted_iota(jnp.int32, (total, total), 0)
    lane = lax.broadcasted_iota(jnp.int32, (total, total), 1)
    bit = 1
    while bit < blocks:
        shift = bit * height
        other = jnp.where(
            (lane // shift) % 2 == 0,
            jnp.roll(counts, -shift, axis=1),
            jnp.roll(counts, shift, axis=1),
        )
        counts = jnp.where((me // bit) % 2 == 1, other, counts)
        bit *= 2
    bias = jnp.where(
        (lax.rem(lane, height) >= rows) & (row != lane),
        jnp.log1p(hardness_multiplier * counts),
        -jnp.inf,
    )
    mine_ref[:rows] = in_order(hit, bias[:rows])
    mine_ref[rows:height] = bias[rows:height]
    mine_ref[height : height + rows] = jnp.concatenate(
        [hit.T, jnp.zeros((rows, total - rows), jnp.float32)], axis=1
    )
    mine_ref[height + rows :] = jnp.concatenate(
        [jnp.zeros((rows, rows), jnp.float32), hit.T, jnp.zeros((rows, total - height), jnp.float32)],
        axis=1,
    )
    turned_ref[...] = bias.T.reshape(blocks, height, total)[:, rows:].reshape(blocks * rows, total)
    block = block_refs[0]
    back = hit.T.astype(jnp.bfloat16)
    anchors = jnp.dot(back, block[0, rows:, :width], preferred_element_type=jnp.float32)
    request_ref[...] = anchors * -scale
    passage_ref[...] = block[0, :rows, :width].astype(jnp.float32) * -scale


def finish_kernel(places, width, pieces, *refs):
    own_ref, other_ref, turned_ref, mine_ref, request_base, passage_base = refs[:6]
    block_refs = refs[6:-7]
    request_hbm, passage_hbm, loss_hbm, request_ref, passage_ref, loss_ref, sems = refs[-7:]
    height, blocks = block_refs[0].shape[1], len(places)
    rows, total = height // 2, blocks * height
    documents = blocks * rows
    scores = (own_ref[...] + other_ref[...]) * scale
    turned = scores[:documents] + turned_ref[...]
    is_document = lax.rem(lax.broadcasted_iota(jnp.int32, (1, total), 1), height) >= rows

    def partner(value):
        return jnp.where(
            is_document, jnp.roll(value, rows, axis=1), jnp.roll(value, -rows, axis=1)
        )

    top = jnp.max(turned, axis=0, keepdims=True)
    top = jnp.maximum(top, partner(top))
    mass = jnp.sum(jnp.exp(turned - top), axis=0, keepdims=True)
    lse = top + jnp.log(mass + partner(mass))
    at = lax.broadcasted_iota(jnp.int32, (rows, total), 1)
    slot = lax.broadcasted_iota(jnp.int32, (rows, total), 0)
    slot_lse = jnp.sum(jnp.where(at == slot, lse, 0.0), axis=1, keepdims=True)
    query_lse = jnp.sum(
        jnp.where(mine_ref[height : height + rows] > 0.0, lse, 0.0), axis=1, keepdims=True
    )
    query_logits = scores[documents:] + mine_ref[:rows]
    query_weights = jnp.exp(query_logits - query_lse)
    document_weights = jnp.exp(scores[:rows] + mine_ref[rows:height] - slot_lse)
    onto = jnp.exp(turned[:rows] - lse)
    left = jnp.concatenate(
        [query_weights, document_weights, onto, jnp.zeros_like(onto)], axis=0
    ).astype(jnp.bfloat16)
    copies = []
    step = width // pieces
    for n in range(pieces):
        span = pl.ds(n * step, step)
        values = stack(block_refs, places, n * step, (n + 1) * step)
        product = jnp.dot(left, values, preferred_element_type=jnp.float32)
        request_ref[:, span] = product[:rows] * scale + request_base[:, span]
        passage_ref[:, span] = (
            product[rows : 2 * rows] + product[2 * rows : 3 * rows]
        ) * scale + passage_base[:, span]
        for k, (source, target) in enumerate(
            ((request_ref, request_hbm), (passage_ref, passage_hbm))
        ):
            copies.append(
                pltpu.make_async_copy(source.at[:, span], target.at[:, span], sems.at[2 * n + k])
            )
            copies[-1].start()
    picked = jnp.sum(
        jnp.where(mine_ref[height + rows :] > 0.0, query_logits, 0.0), axis=1, keepdims=True
    )
    loss_ref[...] = jnp.sum(jnp.where(at == slot, query_lse - picked, 0.0), axis=0)[:rows]
    copies.append(pltpu.make_async_copy(loss_ref, loss_hbm, sems.at[2 * pieces]))
    copies[-1].start()
    for copy in copies:
        copy.wait()


def exchange(value, mask):
    return lax.ppermute(value, "row", [(i, i ^ mask) for i in range(lax.axis_size("row"))])


PIECES = 4
READS = 2
PLAN = (((0,), 4), ((0,), 2), ((0,), 1), ((0, 1), 3), ((1,), 1), ((1,), 2))


def on_device_fast(queries, documents, positive, hard_ids):
    rows, width = queries.shape
    count = lax.axis_size("row")
    height, total = 2 * rows, 2 * rows * count
    tail = -(-total // LANES) * LANES
    block, hit = pl.pallas_call(
        pack_kernel,
        out_shape=(
            jax.ShapeDtypeStruct((height, width + tail), jnp.bfloat16),
            jax.ShapeDtypeStruct((rows, rows), jnp.float32),
        ),
        in_specs=[HBM, HBM, HBM, HBM],
        out_specs=(VMEM, VMEM),
        scratch_shapes=[
            pltpu.SMEM(positive.shape, positive.dtype),
            pltpu.VMEM(queries.shape, queries.dtype),
            pltpu.VMEM(documents.shape, documents.dtype),
            pltpu.VMEM(hard_ids.shape, hard_ids.dtype),
            pltpu.SemaphoreType.DMA((2 + 2 * READS,)),
        ],
        compiler_params=PARAMS,
        name="pack",
    )(*(pltpu.with_memory_space_constraint(v, pltpu.HBM) for v in (positive, queries, documents, hard_ids)))
    pieces, distances = [block[None]], [[0]]
    for sources, mask in PLAN:
        held = [pieces[n] for n in sources]
        held = held[0] if len(held) == 1 else jnp.concatenate(held, axis=0)
        pieces.append(exchange(held, mask))
        distances.append([m ^ mask for n in sources for m in distances[n]])
    where = {m: (p, n) for p, found in enumerate(distances) for n, m in enumerate(found)}
    places = [where[m] for m in range(count)]
    own = pl.pallas_call(
        functools.partial(score_kernel, places, width),
        out_shape=jax.ShapeDtypeStruct((total // 2 + rows, total), jnp.float32),
        in_specs=[VMEM] * (1 + len(pieces)),
        out_specs=VMEM,
        compiler_params=PARAMS,
        name="score",
    )(hit, *pieces)
    other = lax.ppermute(own, "col", [(0, 1), (1, 0)])
    prepared = pl.pallas_call(
        functools.partial(bias_kernel, places, width),
        out_shape=(
            jax.ShapeDtypeStruct((total // 2, total), jnp.float32),
            jax.ShapeDtypeStruct((2 * height, total), jnp.float32),
            jax.ShapeDtypeStruct((rows, width), jnp.float32),
            jax.ShapeDtypeStruct((rows, width), jnp.float32),
        ),
        in_specs=[VMEM] * (1 + len(pieces)),
        out_specs=(VMEM, VMEM, VMEM, VMEM),
        compiler_params=PARAMS,
        name="bias",
    )(hit, *pieces)
    return pl.pallas_call(
        functools.partial(finish_kernel, places, width, PIECES),
        out_shape=(
            jax.ShapeDtypeStruct((rows, width), jnp.float32),
            jax.ShapeDtypeStruct((rows, width), jnp.float32),
            jax.ShapeDtypeStruct((rows,), jnp.float32),
        ),
        in_specs=[VMEM] * (6 + len(pieces)),
        out_specs=(HBM, HBM, HBM),
        scratch_shapes=[
            pltpu.VMEM((rows, width), jnp.float32),
            pltpu.VMEM((rows, width), jnp.float32),
            pltpu.VMEM((rows,), jnp.float32),
            pltpu.SemaphoreType.DMA((2 * PIECES + 1,)),
        ],
        compiler_params=PARAMS,
        name="finish",
    )(own, other, *prepared, *pieces)


def weigh(request_similarity, passage_similarity, positive, hard_ids, batch_size):
    columns = jnp.arange(batch_size, dtype=jnp.int32)
    hardness_tally = jnp.zeros(request_similarity.shape, jnp.float32)
    for column in range(hard_ids.shape[1]):
        hardness_tally = hardness_tally + (hard_ids[:, column][:, None] == columns[None, :]).astype(
            jnp.float32
        )
    request_raw_similarity = request_similarity / sharpness_divisor + jnp.log1p(
        hardness_multiplier * hardness_tally
    )
    matching_indicator = positive[:, None] == columns[None, :]
    passage_raw_similarity = jnp.where(
        matching_indicator, -jnp.inf, passage_similarity / sharpness_divisor
    )
    row_peak = jnp.maximum(
        jnp.max(request_raw_similarity, axis=1), jnp.max(passage_raw_similarity, axis=1)
    )
    row_mass = jnp.sum(jnp.exp(request_raw_similarity - row_peak[:, None]), axis=1) + jnp.sum(
        jnp.exp(passage_raw_similarity - row_peak[:, None]), axis=1
    )
    row_lse = row_peak + jnp.log(row_mass)
    loss_rows = row_lse - jnp.sum(
        jnp.where(matching_indicator, request_raw_similarity, 0.0), axis=1
    )
    request_probability = jnp.exp(request_raw_similarity - row_lse[:, None]).astype(jnp.bfloat16)
    passage_probability = jnp.exp(passage_raw_similarity - row_lse[:, None]).astype(jnp.bfloat16)
    return (request_probability, passage_probability, loss_rows)


def contract_first(left, right):
    return lax.dot_general(
        left, right, (((0,), (0,)), ((), ())), preferred_element_type=jnp.float32
    )


def on_device_wide(queries, documents, positive, hard_ids):
    row_count = queries.shape[0]
    batch_size = row_count * lax.axis_size("row")
    offset = lax.axis_index("row") * row_count
    request_matrix = queries.astype(jnp.bfloat16)
    passage_matrix = documents.astype(jnp.bfloat16)
    local_pos = positive - offset
    picker = local_pos[:, None] == jnp.arange(row_count, dtype=jnp.int32)[None, :]
    reference_side_entries = jnp.take(passage_matrix, local_pos, axis=0)
    document_gathered, query_all = (
        lax.all_gather(passage_matrix, "row", axis=0, tiled=True),
        lax.all_gather(request_matrix, "row", axis=0, tiled=True),
    )
    stacked = jnp.concatenate([request_matrix, reference_side_entries], axis=0)
    partial_value = lax.dot_general(
        stacked, document_gathered, (((1,), (1,)), ((), ())), preferred_element_type=jnp.float32
    )
    query_part = partial_value[:row_count]
    doc_part = partial_value[row_count:]
    request_similarity, passage_similarity = lax.psum((query_part, doc_part), "col")
    request_probability, passage_probability, loss_rows = weigh(
        request_similarity, passage_similarity, positive, hard_ids, batch_size
    )
    request_derivative = (
        jnp.dot(request_probability, document_gathered, preferred_element_type=jnp.float32)
        - reference_side_entries.astype(jnp.float32)
    ) / sharpness_divisor
    reference_side_derivative = (
        jnp.dot(passage_probability, document_gathered, preferred_element_type=jnp.float32)
        / sharpness_divisor
    )
    forwarded_entries = (
        reference_side_derivative - request_matrix.astype(jnp.float32) / sharpness_divisor
    )
    permuted = contract_first(picker.astype(jnp.bfloat16), passage_probability).astype(jnp.bfloat16)
    query_columns, anchor_columns = (
        lax.all_to_all(request_probability, "row", split_axis=1, concat_axis=0, tiled=True),
        lax.all_to_all(permuted, "row", split_axis=1, concat_axis=0, tiled=True),
    )
    anchor_contribution = contract_first(anchor_columns, document_gathered)
    query_contribution = contract_first(query_columns, query_all)
    dispersion_level = lax.dot_general(
        picker.astype(jnp.float32),
        forwarded_entries,
        (((0,), (0,)), ((), ())),
        precision=lax.Precision.HIGHEST,
        preferred_element_type=jnp.float32,
    )
    passage_derivative = (
        query_contribution + anchor_contribution
    ) / sharpness_divisor + dispersion_level
    return (request_derivative, passage_derivative, loss_rows)


def solution(mesh):
    small = mesh.shape["row"] == 8 and mesh.shape["col"] == 2
    return jax.shard_map(
        on_device_fast if small else on_device_wide,
        mesh=mesh,
        in_specs=(
            P(("groups", "row"), "col"),
            P(("groups", "row"), "col"),
            P(("groups", "row")),
            P(("groups", "row"), None),
        ),
        out_specs=(P(("groups", "row"), "col"), P(("groups", "row"), "col"), P(("groups", "row"))),
        check_vma=False,
    )
```

```python
import functools

import jax
import jax.numpy as jnp
from jax import lax
from jax.experimental import pallas as pl
from jax.experimental.pallas import tpu as pltpu
from jax.sharding import PartitionSpec as P


sharpness_divisor = 0.05
hardness_multiplier = 3.0
scale = 1.0 / sharpness_divisor
LANES = 128
VMEM = pl.BlockSpec(memory_space=pltpu.VMEM)
SMEM = pl.BlockSpec(memory_space=pltpu.SMEM)
HBM = pl.BlockSpec(memory_space=pltpu.HBM)
PARAMS = pltpu.CompilerParams(vmem_limit_bytes=8 << 20)


def slot_matrix(positive_ref, rows):
    slots = lax.broadcasted_iota(jnp.int32, (rows, rows), 0)
    places = lax.broadcasted_iota(jnp.int32, (rows, rows), 1)
    hit = jnp.zeros((rows, rows), jnp.float32)
    for i in range(rows):
        local = lax.rem(positive_ref[i], rows)
        hit = jnp.where((places == i) & (slots == local), 1.0, hit)
    return hit


def pack_kernel(
    positive_hbm,
    query_hbm,
    doc_hbm,
    hard_hbm,
    out_ref,
    hit_ref,
    positive_ref,
    query_ref,
    doc_ref,
    hard_ref,
    sems,
):
    rows, width = query_ref.shape
    tail = out_ref.shape[1] - 2 * width
    step = width // READS
    spans = [pl.ds(n * step, step) for n in range(READS)]
    pairs = [(positive_hbm, positive_ref), (hard_hbm, hard_ref)]
    for span in spans:
        pairs.append((query_hbm.at[:, span], query_ref.at[:, span]))
        pairs.append((doc_hbm.at[:, span], doc_ref.at[:, span]))
    copies = [
        pltpu.make_async_copy(source, target, sems.at[n]) for n, (source, target) in enumerate(pairs)
    ]
    for copy in copies:
        copy.start()
    copies[0].wait()
    copies[1].wait()
    hit = slot_matrix(positive_ref, rows)
    hit_ref[...] = hit
    chosen = [hit[:, i][:, None] > 0.0 for i in range(rows)]

    def in_slots(value):
        placed = jnp.zeros_like(value)
        for i in range(rows):
            placed = jnp.where(chosen[i], value[i][None, :], placed)
        return placed

    lane = lax.broadcasted_iota(jnp.int32, (rows, tail), 1)
    block, place = lane // (2 * rows), lax.rem(lane, 2 * rows)
    column = jnp.where(place >= rows, block * rows + place - rows, -1)
    hard = hard_ref[...]
    counts = jnp.zeros((rows, tail), jnp.float32)
    for k in range(hard.shape[1]):
        counts = counts + jnp.where(hard[:, k][:, None] == column, 1.0, 0.0)
    out_ref[:, 2 * width :] = in_slots(counts).astype(jnp.bfloat16)
    for n, span in enumerate(spans):
        copies[2 + 2 * n].wait()
        copies[3 + 2 * n].wait()
        out_ref[:, span] = in_slots(query_ref[:, span]).astype(jnp.bfloat16)
        out_ref[:, pl.ds(width + n * step, step)] = doc_ref[:, span].astype(jnp.bfloat16)


def stack(refs, places, width, start, stop):
    halves = []
    for p, n in places:
        halves.append(refs[p][n, :, start:stop])
        halves.append(refs[p][n, :, width + start : width + stop])
    return jnp.concatenate(halves, axis=0)


def in_order(hit, value):
    back = hit.T
    placed = jnp.zeros_like(value)
    for p in range(value.shape[0]):
        placed = jnp.where(back[:, p][:, None] > 0.0, value[p][None, :], placed)
    return placed


def score_kernel(places, width, hit_ref, *refs):
    *block_refs, score_ref = refs
    values = stack(block_refs, places, width, 0, width)
    product = lax.dot_general(
        values, values, (((1,), (1,)), ((), ())), preferred_element_type=jnp.float32
    )
    height, blocks = 2 * block_refs[0].shape[1], len(places)
    rows = height // 2
    by_block = product.reshape(blocks, height, blocks * height)
    score_ref[: blocks * rows] = by_block[:, rows:].reshape(blocks * rows, blocks * height)
    score_ref[blocks * rows :] = in_order(hit_ref[...], product[:rows])


def bias_kernel(places, width, hit_ref, *refs):
    *block_refs, turned_ref, mine_ref, request_ref, passage_ref = refs
    hit = hit_ref[...]
    me = lax.axis_index("row")
    height, blocks = 2 * block_refs[0].shape[1], len(places)
    rows, total = height // 2, blocks * height
    counts = []
    for p, n in places:
        counts.append(block_refs[p][n, :, 2 * width : 2 * width + total].astype(jnp.float32))
        counts.append(jnp.zeros_like(counts[-1]))
    counts = jnp.concatenate(counts, axis=0)
    row = lax.broadcasted_iota(jnp.int32, (total, total), 0)
    lane = lax.broadcasted_iota(jnp.int32, (total, total), 1)
    bit = 1
    while bit < blocks:
        shift = bit * height
        other = jnp.where(
            (lane // shift) % 2 == 0,
            jnp.roll(counts, -shift, axis=1),
            jnp.roll(counts, shift, axis=1),
        )
        counts = jnp.where((me // bit) % 2 == 1, other, counts)
        bit *= 2
    bias = jnp.where(
        (lax.rem(lane, height) >= rows) & (row != lane),
        jnp.log1p(hardness_multiplier * counts),
        -jnp.inf,
    )
    mine_ref[:rows] = in_order(hit, bias[:rows])
    mine_ref[rows:height] = bias[rows:height]
    mine_ref[height : height + rows] = jnp.concatenate(
        [hit.T, jnp.zeros((rows, total - rows), jnp.float32)], axis=1
    )
    mine_ref[height + rows :] = jnp.concatenate(
        [jnp.zeros((rows, rows), jnp.float32), hit.T, jnp.zeros((rows, total - height), jnp.float32)],
        axis=1,
    )
    turned_ref[...] = bias.T.reshape(blocks, height, total)[:, rows:].reshape(blocks * rows, total)
    block = block_refs[0]
    back = hit.T.astype(jnp.bfloat16)
    anchors = jnp.dot(back, block[0, :, width : 2 * width], preferred_element_type=jnp.float32)
    request_ref[...] = anchors * -scale
    passage_ref[...] = block[0, :, :width].astype(jnp.float32) * -scale


def finish_kernel(places, width, pieces, *refs):
    own_ref, other_ref, turned_ref, mine_ref, request_base, passage_base = refs[:6]
    block_refs = refs[6:-7]
    request_hbm, passage_hbm, loss_hbm, request_ref, passage_ref, loss_ref, sems = refs[-7:]
    height, blocks = 2 * block_refs[0].shape[1], len(places)
    rows, total = height // 2, blocks * height
    documents = blocks * rows
    scores = (own_ref[...] + other_ref[...]) * scale
    turned = scores[:documents] + turned_ref[...]
    is_document = lax.rem(lax.broadcasted_iota(jnp.int32, (1, total), 1), height) >= rows

    def partner(value):
        return jnp.where(
            is_document, jnp.roll(value, rows, axis=1), jnp.roll(value, -rows, axis=1)
        )

    top = jnp.max(turned, axis=0, keepdims=True)
    top = jnp.maximum(top, partner(top))
    mass = jnp.sum(jnp.exp(turned - top), axis=0, keepdims=True)
    lse = top + jnp.log(mass + partner(mass))
    at = lax.broadcasted_iota(jnp.int32, (rows, total), 1)
    slot = lax.broadcasted_iota(jnp.int32, (rows, total), 0)
    slot_lse = jnp.sum(jnp.where(at == slot, lse, 0.0), axis=1, keepdims=True)
    query_lse = jnp.sum(
        jnp.where(mine_ref[height : height + rows] > 0.0, lse, 0.0), axis=1, keepdims=True
    )
    query_logits = scores[documents:] + mine_ref[:rows]
    query_weights = jnp.exp(query_logits - query_lse)
    document_weights = jnp.exp(scores[:rows] + mine_ref[rows:height] - slot_lse)
    onto = jnp.exp(turned[:rows] - lse)
    left = jnp.concatenate(
        [query_weights, document_weights, onto, jnp.zeros_like(onto)], axis=0
    ).astype(jnp.bfloat16)
    copies = []
    step = width // pieces
    for n in range(pieces):
        span = pl.ds(n * step, step)
        values = stack(block_refs, places, width, n * step, (n + 1) * step)
        product = jnp.dot(left, values, preferred_element_type=jnp.float32)
        request_ref[:, span] = product[:rows] * scale + request_base[:, span]
        passage_ref[:, span] = (
            product[rows : 2 * rows] + product[2 * rows : 3 * rows]
        ) * scale + passage_base[:, span]
        for k, (source, target) in enumerate(
            ((request_ref, request_hbm), (passage_ref, passage_hbm))
        ):
            copies.append(
                pltpu.make_async_copy(source.at[:, span], target.at[:, span], sems.at[2 * n + k])
            )
            copies[-1].start()
    picked = jnp.sum(
        jnp.where(mine_ref[height + rows :] > 0.0, query_logits, 0.0), axis=1, keepdims=True
    )
    loss_ref[...] = jnp.sum(jnp.where(at == slot, query_lse - picked, 0.0), axis=0)[:rows]
    copies.append(pltpu.make_async_copy(loss_ref, loss_hbm, sems.at[2 * pieces]))
    copies[-1].start()
    for copy in copies:
        copy.wait()


def exchange(value, mask):
    return lax.ppermute(value, "row", [(i, i ^ mask) for i in range(lax.axis_size("row"))])


PIECES = 4
READS = 2
PLAN = (((0,), 4), ((0,), 2), ((0,), 3), ((0, 1), 1), ((1,), 3), ((1,), 2))


def on_device_fast(queries, documents, positive, hard_ids):
    rows, width = queries.shape
    count = lax.axis_size("row")
    height, total = 2 * rows, 2 * rows * count
    tail = -(-total // LANES) * LANES
    block, hit = pl.pallas_call(
        pack_kernel,
        out_shape=(
            jax.ShapeDtypeStruct((rows, 2 * width + tail), jnp.bfloat16),
            jax.ShapeDtypeStruct((rows, rows), jnp.float32),
        ),
        in_specs=[HBM, HBM, HBM, HBM],
        out_specs=(VMEM, VMEM),
        scratch_shapes=[
            pltpu.SMEM(positive.shape, positive.dtype),
            pltpu.VMEM(queries.shape, queries.dtype),
            pltpu.VMEM(documents.shape, documents.dtype),
            pltpu.VMEM(hard_ids.shape, hard_ids.dtype),
            pltpu.SemaphoreType.DMA((2 + 2 * READS,)),
        ],
        compiler_params=PARAMS,
        name="pack",
    )(*(pltpu.with_memory_space_constraint(v, pltpu.HBM) for v in (positive, queries, documents, hard_ids)))
    pieces, distances = [block[None]], [[0]]
    for sources, mask in PLAN:
        held = [pieces[n] for n in sources]
        held = held[0] if len(held) == 1 else jnp.concatenate(held, axis=0)
        pieces.append(exchange(held, mask))
        distances.append([m ^ mask for n in sources for m in distances[n]])
    where = {m: (p, n) for p, found in enumerate(distances) for n, m in enumerate(found)}
    places = [where[m] for m in range(count)]
    own = pl.pallas_call(
        functools.partial(score_kernel, places, width),
        out_shape=jax.ShapeDtypeStruct((total // 2 + rows, total), jnp.float32),
        in_specs=[VMEM] * (1 + len(pieces)),
        out_specs=VMEM,
        compiler_params=PARAMS,
        name="score",
    )(hit, *pieces)
    other = lax.ppermute(own, "col", [(0, 1), (1, 0)])
    prepared = pl.pallas_call(
        functools.partial(bias_kernel, places, width),
        out_shape=(
            jax.ShapeDtypeStruct((total // 2, total), jnp.float32),
            jax.ShapeDtypeStruct((2 * height, total), jnp.float32),
            jax.ShapeDtypeStruct((rows, width), jnp.float32),
            jax.ShapeDtypeStruct((rows, width), jnp.float32),
        ),
        in_specs=[VMEM] * (1 + len(pieces)),
        out_specs=(VMEM, VMEM, VMEM, VMEM),
        compiler_params=PARAMS,
        name="bias",
    )(hit, *pieces)
    return pl.pallas_call(
        functools.partial(finish_kernel, places, width, PIECES),
        out_shape=(
            jax.ShapeDtypeStruct((rows, width), jnp.float32),
            jax.ShapeDtypeStruct((rows, width), jnp.float32),
            jax.ShapeDtypeStruct((rows,), jnp.float32),
        ),
        in_specs=[VMEM] * (6 + len(pieces)),
        out_specs=(HBM, HBM, HBM),
        scratch_shapes=[
            pltpu.VMEM((rows, width), jnp.float32),
            pltpu.VMEM((rows, width), jnp.float32),
            pltpu.VMEM((rows,), jnp.float32),
            pltpu.SemaphoreType.DMA((2 * PIECES + 1,)),
        ],
        compiler_params=PARAMS,
        name="finish",
    )(own, other, *prepared, *pieces)


def weigh(request_similarity, passage_similarity, positive, hard_ids, batch_size):
    columns = jnp.arange(batch_size, dtype=jnp.int32)
    hardness_tally = jnp.zeros(request_similarity.shape, jnp.float32)
    for column in range(hard_ids.shape[1]):
        hardness_tally = hardness_tally + (hard_ids[:, column][:, None] == columns[None, :]).astype(
            jnp.float32
        )
    request_raw_similarity = request_similarity / sharpness_divisor + jnp.log1p(
        hardness_multiplier * hardness_tally
    )
    matching_indicator = positive[:, None] == columns[None, :]
    passage_raw_similarity = jnp.where(
        matching_indicator, -jnp.inf, passage_similarity / sharpness_divisor
    )
    row_peak = jnp.maximum(
        jnp.max(request_raw_similarity, axis=1), jnp.max(passage_raw_similarity, axis=1)
    )
    row_mass = jnp.sum(jnp.exp(request_raw_similarity - row_peak[:, None]), axis=1) + jnp.sum(
        jnp.exp(passage_raw_similarity - row_peak[:, None]), axis=1
    )
    row_lse = row_peak + jnp.log(row_mass)
    loss_rows = row_lse - jnp.sum(
        jnp.where(matching_indicator, request_raw_similarity, 0.0), axis=1
    )
    request_probability = jnp.exp(request_raw_similarity - row_lse[:, None]).astype(jnp.bfloat16)
    passage_probability = jnp.exp(passage_raw_similarity - row_lse[:, None]).astype(jnp.bfloat16)
    return (request_probability, passage_probability, loss_rows)


def contract_first(left, right):
    return lax.dot_general(
        left, right, (((0,), (0,)), ((), ())), preferred_element_type=jnp.float32
    )


def on_device_wide(queries, documents, positive, hard_ids):
    row_count = queries.shape[0]
    batch_size = row_count * lax.axis_size("row")
    offset = lax.axis_index("row") * row_count
    request_matrix = queries.astype(jnp.bfloat16)
    passage_matrix = documents.astype(jnp.bfloat16)
    local_pos = positive - offset
    picker = local_pos[:, None] == jnp.arange(row_count, dtype=jnp.int32)[None, :]
    reference_side_entries = jnp.take(passage_matrix, local_pos, axis=0)
    document_gathered, query_all = (
        lax.all_gather(passage_matrix, "row", axis=0, tiled=True),
        lax.all_gather(request_matrix, "row", axis=0, tiled=True),
    )
    stacked = jnp.concatenate([request_matrix, reference_side_entries], axis=0)
    partial_value = lax.dot_general(
        stacked, document_gathered, (((1,), (1,)), ((), ())), preferred_element_type=jnp.float32
    )
    query_part = partial_value[:row_count]
    doc_part = partial_value[row_count:]
    request_similarity, passage_similarity = lax.psum((query_part, doc_part), "col")
    request_probability, passage_probability, loss_rows = weigh(
        request_similarity, passage_similarity, positive, hard_ids, batch_size
    )
    request_derivative = (
        jnp.dot(request_probability, document_gathered, preferred_element_type=jnp.float32)
        - reference_side_entries.astype(jnp.float32)
    ) / sharpness_divisor
    reference_side_derivative = (
        jnp.dot(passage_probability, document_gathered, preferred_element_type=jnp.float32)
        / sharpness_divisor
    )
    forwarded_entries = (
        reference_side_derivative - request_matrix.astype(jnp.float32) / sharpness_divisor
    )
    permuted = contract_first(picker.astype(jnp.bfloat16), passage_probability).astype(jnp.bfloat16)
    query_columns, anchor_columns = (
        lax.all_to_all(request_probability, "row", split_axis=1, concat_axis=0, tiled=True),
        lax.all_to_all(permuted, "row", split_axis=1, concat_axis=0, tiled=True),
    )
    anchor_contribution = contract_first(anchor_columns, document_gathered)
    query_contribution = contract_first(query_columns, query_all)
    dispersion_level = lax.dot_general(
        picker.astype(jnp.float32),
        forwarded_entries,
        (((0,), (0,)), ((), ())),
        precision=lax.Precision.HIGHEST,
        preferred_element_type=jnp.float32,
    )
    passage_derivative = (
        query_contribution + anchor_contribution
    ) / sharpness_divisor + dispersion_level
    return (request_derivative, passage_derivative, loss_rows)


def solution(mesh):
    small = mesh.shape["row"] == 8 and mesh.shape["col"] == 2
    return jax.shard_map(
        on_device_fast if small else on_device_wide,
        mesh=mesh,
        in_specs=(
            P(("groups", "row"), "col"),
            P(("groups", "row"), "col"),
            P(("groups", "row")),
            P(("groups", "row"), None),
        ),
        out_specs=(P(("groups", "row"), "col"), P(("groups", "row"), "col"), P(("groups", "row"))),
        check_vma=False,
    )
```
